32 devices in a mesh: dx: 4 (over y, x), dy: 8 (over z, core).
Axes of the slice: x: 2, y: 2, z: 4, core: 2. Of those that a mesh axis runs over, the one named last changes fastest.
Arguments:
- audio: bfloat16 [8, 32, 2570], P('dy', 'dx'), may hold values from -6 to 6
- counts: int32 [8, 4], P('dy', 'dx'), may hold values from 1 to 8, 16 in all within a row
- cotangent: bfloat16 [8, 16, 256, 512], P('dy', 'dx'), may hold values from -6 to 6
- conv_first: bfloat16 [10, 512], replicated, may hold values from -2 to 2
- norm_gain: float32 [512], replicated, may hold values from 0.1 to 1.9
- norm_bias: float32 [512], replicated, may hold values from -3 to 3
- conv_second: bfloat16 [1536, 512], replicated, may hold values from -0.15625 to 0.15625
Outputs:
- grad_conv_first: float32 [10, 512], replicated
- grad_norm: float32 [2, 512], replicated
- grad_conv_second: float32 [1536, 512], P('dy')
The draws below stay inside these ranges and needn't reach their ends.
Inputs may be any that keep to these rules, and one draw needn't show every extreme that they name: In each group along dy the counts sum to 16, and some device of each group holds exactly 8 live crops.
All inputs are finite; a program needn't handle non-finite values.
Results may differ from the reference program's by a relative error of at most 0.0051.
Values may be sent and summed in bfloat16 or wider, within the bound.
No kernel may reach another device: no remote copies, remote signals or barrier semaphores. Data moves between devices by JAX's collectives and lax.ppermute only.
A program may use at most 128 MiB of HBM per device.

```python
import math
import jax
import jax.numpy as jnp
import numpy as np
from jax import lax

C = 512
RECV = 4
T2 = 256
SLOTS = 8
CROP = 2570
CROPS = 16
GROUPS = 8
PEERS = 4


def block_scale(stream_key, shape, pieces, low, top_value):
    def one(position, shards_of):
        draws = jax.random.uniform(jax.random.fold_in(jax.random.fold_in(stream_key, 6), position), (shards_of,), jnp.float32, low / len(pieces), top_value / len(pieces))
        return jnp.repeat(jnp.exp(draws), shape[position] // shards_of).reshape((-1,) + (1,) * (len(shape) - position - 1))

    loudness = one(*pieces[0])
    for cut in pieces[1:]:
        loudness = loudness * one(*cut)
    return loudness


def split_up(number_of, total, reach, slope):
    loads = [(1 << 20) // math.isqrt(standing ** slope) + 1 for standing in range(2, number_of + 1)]
    rest, given = total - reach - (number_of - 1), [1] * (number_of - 1)
    while rest > 0:
        movable = [i for i in range(number_of - 1) if given[i] < reach]
        whole, left = sum([loads[i] for i in movable]), rest
        for i in movable:
            extra = min(reach - given[i], max(1, left * loads[i] // whole), rest)
            given[i] = given[i] + extra
            rest = rest - extra
    return np.array([reach] + given)


def ragged_sizes(rng, number_of, total, reach, skew):
    if number_of == 2:
        one = jax.random.randint(rng, (), max(1, total - reach), min(reach, total - 1) + 1)
        return jnp.stack([one, total - one])
    lengths = jnp.asarray(split_up(number_of, total, reach, skew), jnp.int32)
    pairs = (number_of - 1) // 2
    giver, receiver = lengths[1:1 + 2 * pairs:2], lengths[2:2 + 2 * pairs:2]
    room = jnp.minimum(giver - 1, reach - receiver)
    passed = jax.random.randint(jax.random.fold_in(rng, 1), (pairs,), 0, 1 << 20) % (room + 1)
    lengths = lengths.at[1:1 + 2 * pairs:2].set(giver - passed).at[2:2 + 2 * pairs:2].set(receiver + passed)
    return lengths[jax.random.permutation(jax.random.fold_in(rng, 2), number_of)]


def scatter_about(stream_key, shape, deviation, most, split=(), kind=jnp.bfloat16):
    gain = block_scale(stream_key, shape, split, -0.22, 0.18) if split else 1.0
    entries = jax.random.normal(stream_key, shape, jnp.float32) * deviation * gain
    return jnp.minimum(jnp.maximum(entries, -most), most).astype(kind)


def setup_inputs(seed: int = 0) -> dict:
    key_list = jax.random.split(jax.random.key(seed), 8)
    return {
        "audio": scatter_about(key_list[0], (GROUPS, PEERS * SLOTS, CROP), 1.0, 6.0, ((0, 8), (1, 4))),
        "counts": jax.vmap(lambda own: ragged_sizes(own, PEERS, CROPS, SLOTS, 2))(jax.random.split(key_list[1], GROUPS)).reshape((GROUPS, PEERS)).astype(jnp.int32),
        "cotangent": scatter_about(key_list[2], (GROUPS, CROPS, T2, C), 1.0, 6.0, ((0, 8), (1, 4))),
        "conv_first": scatter_about(key_list[3], (10, C), 10 ** -0.5, 2.0),
        "norm_gain": jnp.clip(1.0 + 0.18 * jax.random.normal(key_list[4], (C,), jnp.float32), 0.1, 1.9),
        "norm_bias": scatter_about(key_list[5], (C,), 0.5, 3.0, (), jnp.float32),
        "conv_second": scatter_about(key_list[6], (3 * C, C), (3 * C) ** -0.5, 0.15625),
    }


def gelu_cdf(value):
    return 0.5 * (1.0 + lax.erf(value * 0.7071067811865476))

def gelu_slope(value):
    return gelu_cdf(value) + value * jnp.exp(-0.5 * value * value) * 0.3989422804014327

def forward_backward(crop_waves, cot_rows, conv_first, norm_gain, norm_bias, conv_second, loss_scale):
    batch_size = crop_waves.shape[0]
    frames = cot_rows.shape[1]
    first_len = 2 * frames + 1
    channels = conv_second.shape[1]
    early_taps = crop_waves[:, :5 * first_len].reshape(batch_size, first_len, 5)
    late_taps = crop_waves[:, 5:5 * first_len + 5].reshape(batch_size, first_len, 5)
    patches = jnp.concatenate([early_taps, late_taps], axis=2).reshape(batch_size * first_len, 10)
    pre_norm = jnp.dot(patches, conv_first, preferred_element_type=jnp.float32).reshape(batch_size, first_len, channels)
    centre = pre_norm - lax.optimization_barrier(jnp.mean(pre_norm, axis=1, keepdims=True))
    inv_std = lax.rsqrt(lax.optimization_barrier(jnp.mean(centre * centre, axis=1, keepdims=True)) + 1e-05)
    normed = centre * inv_std
    shifted = normed * norm_gain + norm_bias
    hidden = (shifted * gelu_cdf(shifted)).astype(jnp.bfloat16)
    two_taps = hidden[:, :2 * frames].reshape(batch_size, frames, 2 * channels)
    third_tap = hidden[:, 2::2]
    second_rows = jnp.concatenate([two_taps, third_tap], axis=2).reshape(batch_size * frames, 3 * channels)
    pre_act = jnp.dot(second_rows, conv_second, preferred_element_type=jnp.float32)
    grad_rows = (loss_scale * cot_rows.reshape(batch_size * frames, channels).astype(jnp.float32) * gelu_slope(pre_act)).astype(jnp.bfloat16)
    grad_cols = jnp.dot(grad_rows, conv_second.T, preferred_element_type=jnp.float32).reshape(batch_size, frames, 3 * channels)
    first_taps = grad_cols[:, :, :2 * channels].reshape(batch_size, 2 * frames, channels)
    late_tap = jnp.stack([grad_cols[:, :, 2 * channels:], jnp.zeros((batch_size, frames, channels), jnp.float32)], axis=2).reshape(batch_size, 2 * frames, channels)
    grad_hidden = jnp.concatenate([first_taps, jnp.zeros((batch_size, 1, channels), jnp.float32)], axis=1)
    grad_hidden = grad_hidden + jnp.concatenate([jnp.zeros((batch_size, 2, channels), jnp.float32), late_tap[:, :2 * frames - 1]], axis=1)
    grad_shift = grad_hidden * gelu_slope(shifted)
    gain_grad = lax.optimization_barrier(jnp.sum(grad_shift * normed, axis=(0, 1)))
    shift_grad = lax.optimization_barrier(jnp.sum(grad_shift, axis=(0, 1)))
    grad_scaled = grad_shift * norm_gain
    grad_pre = inv_std * (grad_scaled - lax.optimization_barrier(jnp.mean(grad_scaled, axis=1, keepdims=True)) - normed * lax.optimization_barrier(jnp.mean(grad_scaled * normed, axis=1, keepdims=True)))
    grad_pre = grad_pre.astype(jnp.bfloat16).reshape(batch_size * first_len, channels)
    grad_first = jnp.dot(patches.T, grad_pre, preferred_element_type=jnp.float32)
    return (second_rows, grad_rows, grad_first, jnp.stack([gain_grad, shift_grad]))

def reference(audio, counts, cotangent, conv_first, norm_gain, norm_bias, conv_second):
    loss_scale = 1.0 / math.sqrt(GROUPS * CROPS * T2)

    def group_step(totals, inputs):
        waves_all, row_counts, row_cot = inputs
        starts = jnp.cumsum(row_counts, dtype=jnp.int32) - row_counts
        positions = jnp.arange(CROPS, dtype=jnp.int32)
        wanted = positions % RECV * PEERS + positions // RECV
        holder = lax.optimization_barrier(jnp.sum((starts[None, :] <= wanted[:, None]).astype(jnp.int32), axis=1, dtype=jnp.int32)) - 1
        offset = wanted - starts[holder]
        crop_waves = jnp.take(waves_all, holder * SLOTS + offset, axis=0)
        second_rows, grad_rows, grad_first, grad_gains = forward_backward(crop_waves, row_cot, conv_first, norm_gain, norm_bias, conv_second, loss_scale)
        grad_second = jnp.dot(second_rows.T, grad_rows, preferred_element_type=jnp.float32)
        updated = (totals[0] + grad_first, totals[1] + grad_gains, totals[2] + grad_second)
        return (updated, None)
    start_sums = (jnp.zeros((10, C), jnp.float32), jnp.zeros((2, C), jnp.float32), jnp.zeros((3 * C, C), jnp.float32))
    totals, unused = lax.scan(group_step, start_sums, (audio, counts, cotangent))
    return (totals[0], totals[1], totals[2])
```

```python
import functools
import math

import jax
import jax.numpy as jnp
from jax import lax
from jax.experimental import pallas as pl
from jax.experimental.pallas import tpu as pltpu
from jax.sharding import PartitionSpec as P

BF16 = jnp.bfloat16
F32 = jnp.float32
LANES = 128
ROWS = 32
VMEM_SPEC = pl.BlockSpec(memory_space=pltpu.VMEM)
SMEM_SPEC = pl.BlockSpec(memory_space=pltpu.SMEM)


def gelu_cdf(value):
    return 0.5 * (1.0 + lax.erf(value * 0.7071067811865476))


def gelu_slope(value):
    return gelu_cdf(value) + value * jnp.exp(-0.5 * value * value) * 0.3989422804014327


def chunk(index, rows=ROWS):
    return pl.ds(pl.multiple_of(index * rows, rows), rows)


def fold(rows):
    total = rows[0:8]
    for start in range(8, rows.shape[0], 8):
        total = total + rows[start : start + 8]
    return total


def forward_kernel(
    peers, slots, crops, frames, channels, block, loss_scale, where, *refs
):
    buffers = refs[:peers]
    (cot, taps, second, gain, bias, keep, send, grad_rows, patches, stats) = refs[
        peers : peers + 10
    ]
    (waves, wave_rows, even, odd, hid, rows, pre, acc) = refs[peers + 10 :]
    crop = pl.program_id(0)
    samples = 10 * (frames + 1)
    first_len = 2 * frames + 1
    own = where[0]
    core = where[1]
    wanted = waves.shape[0]

    @pl.when(crop == 0)
    def _():
        counts = [buffer[0:1, samples : samples + 1].astype(F32) for buffer in buffers]
        slot = lax.broadcasted_iota(jnp.int32, (wanted, slots), 1)
        number = lax.broadcasted_iota(jnp.int32, (wanted, slots), 0) * peers + own
        picked = jnp.zeros(waves.shape, F32)
        for k in range(peers):
            holder = jnp.bitwise_xor(own, k)
            start = jnp.zeros((1, 1), F32)
            for other in range(peers):
                before = jnp.bitwise_xor(own, other) < holder
                start = start + jnp.where(before, counts[other], 0.0)
            first = jnp.broadcast_to(start.astype(jnp.int32), (wanted, slots))
            live = jnp.broadcast_to(counts[k].astype(jnp.int32), (wanted, slots))
            hit = (first + slot == number) & (slot < live)
            one_hot = jnp.where(hit, 1.0, 0.0).astype(BF16)
            picked = picked + jnp.dot(
                one_hot, buffers[k][...], preferred_element_type=F32
            )
        waves[...] = picked
        acc[...] = jnp.zeros_like(acc)

    period = 5 * LANES
    per_block = period // 10
    at = lax.broadcasted_iota(jnp.int32, (period, LANES), 0) % 10
    spread = jnp.where(
        at == lax.broadcasted_iota(jnp.int32, (period, LANES), 1), 1.0, 0.0
    ).astype(BF16)
    lane = lax.broadcasted_iota(jnp.int32, (per_block, period), 1)
    low = lax.broadcasted_iota(jnp.int32, (per_block, period), 0) * 10
    mask = (lane >= low) & (lane < low + 10)
    wave = waves[pl.ds(crop, 1), :]
    for part in range(10 * frames // period):
        piece = jnp.broadcast_to(
            wave[:, part * period : (part + 1) * period], (per_block, period)
        )
        piece = jnp.where(mask, piece, 0.0).astype(BF16)
        wave_rows[part * per_block : (part + 1) * per_block] = jnp.dot(
            piece, spread, preferred_element_type=F32
        )
    last = jnp.broadcast_to(wave[:, 10 * frames : 10 * frames + LANES], (16, LANES))
    last_row = lax.broadcasted_iota(jnp.int32, (16, LANES), 0)
    last_lane = lax.broadcasted_iota(jnp.int32, (16, LANES), 1)
    wave_rows[frames : frames + 16] = jnp.where((last_row == 0) & (last_lane < 10), last, 0.0)
    long = frames + 8
    both = wave_rows[0:long] + pltpu.roll(wave_rows[1 : long + 1], 10, 1)
    patch = both.astype(BF16)
    patches[0] = patch

    first = jnp.dot(patch, taps[:, :channels], preferred_element_type=F32)
    even[...] = first
    total = fold(first)
    first = jnp.dot(patch[:frames], taps[:, channels:], preferred_element_type=F32)
    odd[...] = first
    total = total + fold(first)
    mean = jnp.sum(total, axis=0, keepdims=True) * (1.0 / first_len)
    tail_row = lax.broadcasted_iota(jnp.int32, (8, channels), 0) == 0

    def squares(i, total):
        a = even[chunk(i)] - mean
        b = odd[chunk(i)] - mean
        return total + fold(a * a + b * b)

    tail = even[frames:long] - mean
    total = lax.fori_loop(
        0, frames // ROWS, squares, jnp.where(tail_row, tail * tail, 0.0), unroll=True
    )
    var = jnp.sum(total, axis=0, keepdims=True) * (1.0 / first_len)
    inv_std = lax.rsqrt(var + 1e-05)
    stats[0, 0:1] = mean
    stats[0, 1:2] = inv_std
    scale = gain[...]
    shift = bias[...]

    def hidden(centre):
        value = centre * inv_std * scale + shift
        return value * gelu_cdf(value)

    def hide(i, carry):
        value = hidden(even[chunk(i)] - mean)
        hid[chunk(i)] = value
        rows[chunk(i), 0:channels] = value.astype(BF16)
        rows[chunk(i), channels : 2 * channels] = hidden(odd[chunk(i)] - mean).astype(BF16)
        return carry

    lax.fori_loop(0, frames // ROWS, hide, 0, unroll=True)
    hid[frames:long] = hidden(tail)
    rows[:, 2 * channels :] = hid[1 : frames + 1].astype(BF16)

    pre[...] = jnp.dot(rows[...], second[...], preferred_element_type=F32)

    def slope(i, carry):
        value = loss_scale * cot[0, chunk(i)].astype(F32) * gelu_slope(pre[chunk(i)])
        grad_rows[0, chunk(i)] = value.astype(BF16)
        return carry

    lax.fori_loop(0, frames // ROWS, slope, 0, unroll=True)
    acc[...] += lax.dot_general(
        rows[...],
        grad_rows[0],
        (((0,), (0,)), ((), ())),
        preferred_element_type=F32,
    )

    @pl.when(crop == crops - 1)
    def _():
        for pair in range(acc.shape[0] // (2 * block)):
            mine = pl.ds(pl.multiple_of((2 * pair + core) * block, block), block)
            theirs = pl.ds(pl.multiple_of((2 * pair + 1 - core) * block, block), block)
            keep[pair * block : (pair + 1) * block] = acc[mine]
            send[pair * block : (pair + 1) * block] = acc[theirs].astype(BF16)


def forward(where, buffers, cot, taps, second, gain, bias, block, loss_scale):
    peers = len(buffers)
    slots, width = buffers[0].shape
    crops, frames, channels = cot.shape
    long = frames + 8
    half = second.shape[0] // 2

    def whole(array):
        return pl.BlockSpec(array.shape, lambda i: (0,) * array.ndim)

    def per_crop(*shape):
        return pl.BlockSpec((1, *shape), lambda i: (i, 0, 0))

    return pl.pallas_call(
        functools.partial(
            forward_kernel, peers, slots, crops, frames, channels, block, loss_scale
        ),
        grid=(crops,),
        in_specs=[
            SMEM_SPEC,
            *[whole(b) for b in buffers],
            per_crop(frames, channels),
            whole(taps),
            whole(second),
            whole(gain),
            whole(bias),
        ],
        out_specs=[
            pl.BlockSpec((half, channels), lambda i: (0, 0)),
            pl.BlockSpec((half, channels), lambda i: (0, 0)),
            per_crop(frames, channels),
            per_crop(long, LANES),
            per_crop(8, channels),
        ],
        out_shape=[
            jax.ShapeDtypeStruct((half, channels), F32),
            jax.ShapeDtypeStruct((half, channels), BF16),
            jax.ShapeDtypeStruct((crops, frames, channels), BF16),
            jax.ShapeDtypeStruct((crops, long, LANES), BF16),
            jax.ShapeDtypeStruct((crops, 8, channels), F32),
        ],
        scratch_shapes=[
            pltpu.VMEM((max(8, crops), width), F32),
            pltpu.VMEM((frames + 16, LANES), F32),
            pltpu.VMEM((long, channels), F32),
            pltpu.VMEM((frames, channels), F32),
            pltpu.VMEM((long, channels), F32),
            pltpu.VMEM((frames, 3 * channels), BF16),
            pltpu.VMEM((frames, channels), F32),
            pltpu.VMEM(second.shape, F32),
        ],
        name="forward",
        compiler_params=pltpu.CompilerParams(vmem_limit_bytes=32 << 20),
    )(where, *buffers, cot, taps, second, gain, bias)


def backward_kernel(
    crops, frames, channels, grad_rows, patches, stats, taps, second, gain, bias,
    small, even, odd, cols, grad_even, grad_odd, late, first_acc, gains_acc,
):
    crop = pl.program_id(0)
    long = frames + 8
    first_len = 2 * frames + 1

    @pl.when(crop == 0)
    def _():
        first_acc[...] = jnp.zeros_like(first_acc)
        gains_acc[...] = jnp.zeros_like(gains_acc)

    patch = patches[0]
    even[...] = jnp.dot(patch, taps[:, :channels], preferred_element_type=F32)
    odd[...] = jnp.dot(patch[:frames], taps[:, channels:], preferred_element_type=F32)
    cols[...] = lax.dot_general(
        grad_rows[0],
        second[: 2 * channels],
        (((1,), (1,)), ((), ())),
        preferred_element_type=F32,
    )
    late[0:8] = jnp.zeros((8, channels), F32)
    late[8 : frames + 8] = lax.dot_general(
        grad_rows[0],
        second[2 * channels :],
        (((1,), (1,)), ((), ())),
        preferred_element_type=F32,
    )
    mean = stats[0, 0:1]
    inv_std = stats[0, 1:2]
    scale = gain[...]
    shift = bias[...]

    def shift_grad(pre_norm, grad_hidden):
        normed = (pre_norm - mean) * inv_std
        grad = grad_hidden * gelu_slope(normed * scale + shift)
        return normed, grad

    def first_pass(i, carry):
        shifts, gains = carry
        normed, grad = shift_grad(
            even[chunk(i)], cols[chunk(i), 0:channels] + late[pl.ds(i * ROWS + 7, ROWS), :]
        )
        even[chunk(i)] = normed
        grad_even[chunk(i)] = grad
        shifts = shifts + fold(grad)
        gains = gains + fold(grad * normed)
        normed, grad = shift_grad(odd[chunk(i)], cols[chunk(i), channels:])
        odd[chunk(i)] = normed
        grad_odd[chunk(i)] = grad
        return shifts + fold(grad), gains + fold(grad * normed)

    tail_row = lax.broadcasted_iota(jnp.int32, (8, channels), 0) == 0
    tail_normed, tail_grad = shift_grad(
        even[frames:long],
        jnp.broadcast_to(late[frames + 7 : frames + 8], (8, channels)),
    )
    tail_grad = jnp.where(tail_row, tail_grad, 0.0)
    carry = (tail_grad, tail_grad * tail_normed)
    for i in range(frames // ROWS):
        carry = first_pass(i, carry)
    shifts = jnp.sum(carry[0], axis=0, keepdims=True)
    gains = jnp.sum(carry[1], axis=0, keepdims=True)
    gains_acc[0:1] += gains
    gains_acc[1:2] += shifts
    shifts = shifts * (1.0 / first_len)
    gains = gains * (1.0 / first_len)
    outer = inv_std * scale

    def grad_pre(grad, normed):
        return (outer * (grad - shifts - normed * gains)).astype(BF16)

    tail_pre = jnp.where(tail_row, outer * (tail_grad - shifts - tail_normed * gains), 0.0)
    grads = [grad_pre(grad_even[chunk(i)], even[chunk(i)]) for i in range(frames // ROWS)]
    whole_even = jnp.concatenate(grads, axis=0)
    grads = [grad_pre(grad_odd[chunk(i)], odd[chunk(i)]) for i in range(frames // ROWS)]
    whole_odd = jnp.concatenate(grads, axis=0)

    def outer_sum(a, b):
        return lax.dot_general(a, b, (((0,), (0,)), ((), ())), preferred_element_type=F32)

    first_acc[0:LANES] += outer_sum(patch[:frames], whole_even) + outer_sum(
        patch[frames:long], tail_pre.astype(BF16)
    )
    first_acc[LANES:] += outer_sum(patch[:frames], whole_odd)

    @pl.when(crop == crops - 1)
    def _():
        small[...] = jnp.zeros_like(small)
        small[0:10] = first_acc[0:10] + first_acc[LANES + 5 : LANES + 15]
        small[10:12] = gains_acc[0:2]


def backward(grad_rows, patches, stats, taps, second, gain, bias):
    crops, frames, channels = grad_rows.shape
    long = frames + 8

    def whole(array):
        return pl.BlockSpec(array.shape, lambda i: (0,) * array.ndim)

    def per_crop(array):
        return pl.BlockSpec((1, *array.shape[1:]), lambda i: (i, 0, 0))

    return pl.pallas_call(
        functools.partial(backward_kernel, crops, frames, channels),
        grid=(crops,),
        in_specs=[
            per_crop(grad_rows),
            per_crop(patches),
            per_crop(stats),
            whole(taps),
            whole(second),
            whole(gain),
            whole(bias),
        ],
        out_specs=pl.BlockSpec((16, channels), lambda i: (0, 0)),
        out_shape=jax.ShapeDtypeStruct((16, channels), F32),
        scratch_shapes=[
            pltpu.VMEM((long, channels), F32),
            pltpu.VMEM((frames, channels), F32),
            pltpu.VMEM((frames, 2 * channels), F32),
            pltpu.VMEM((frames, channels), F32),
            pltpu.VMEM((frames, channels), F32),
            pltpu.VMEM((long, channels), F32),
            pltpu.VMEM((2 * LANES, channels), F32),
            pltpu.VMEM((8, channels), F32),
        ],
        name="backward",
        compiler_params=pltpu.CompilerParams(vmem_limit_bytes=32 << 20),
    )(grad_rows, patches, stats, taps, second, gain, bias)


def tree(values):
    while len(values) > 1:
        values = [values[i] + values[i + 1] for i in range(0, len(values), 2)]
    return values[0]


def swap(value, axis, key):
    return lax.ppermute(value, axis, [(i, i ^ key) for i in range(lax.axis_size(axis))])


def parts(value):
    high = value.astype(BF16)
    low = (value - high.astype(F32)).astype(BF16)
    return high, low


def kernel_call(kernel, where, arrays, out_shape, name):
    return pl.pallas_call(
        kernel,
        in_specs=[SMEM_SPEC] + [VMEM_SPEC] * len(arrays),
        out_specs=jax.tree.map(lambda _: VMEM_SPEC, out_shape),
        out_shape=out_shape,
        name=name,
    )(where, *arrays)


def split_dx(where, keep, received, peers, block):
    half, channels = keep.shape
    groups = half // block
    rows = block // peers
    if rows % 16:
        total = (keep + received.astype(F32)).reshape(groups, peers, rows, channels)
        picked = [
            lax.dynamic_index_in_dim(total, where[0] ^ k, axis=1, keepdims=False)
            for k in range(peers)
        ]
        picked = [p.reshape(groups * rows, channels) for p in picked]
        return [picked[0]] + [p.astype(BF16) for p in picked[1:]]

    def body(where, keep, received, *outs):
        for k in range(peers):
            part = jnp.bitwise_xor(where[0], k)
            for g in range(groups):
                at = pl.ds(pl.multiple_of(g * block + part * rows, rows), rows)
                value = keep[at] + received[at].astype(F32)
                outs[k][g * rows : (g + 1) * rows] = value.astype(outs[k].dtype)

    shape = (groups * rows, channels)
    return kernel_call(
        body,
        where,
        (keep, received),
        [jax.ShapeDtypeStruct(shape, BF16 if k else F32) for k in range(peers)],
        "split_dx",
    )


def split_dy(where, own, received, small, small_received, groups):
    rows = own.shape[0] // groups
    channels = own.shape[1]
    extra = small.shape[0]
    if rows % 16:
        total = tree([own] + [r.astype(F32) for r in received])
        total = total.reshape(groups, rows, channels)
        high, low = parts(small + small_received)
        picked = [
            lax.dynamic_index_in_dim(total, where[2] ^ k, axis=0, keepdims=False)
            for k in range(groups)
        ]
        first = jnp.concatenate([picked[0], high.astype(F32), low.astype(F32)], axis=0)
        return [first] + [
            jnp.concatenate([p.astype(BF16), high, low], axis=0) for p in picked[1:]
        ]

    def body(where, own, small, small_received, *refs):
        received, outs = refs[: len(refs) - groups], refs[len(refs) - groups :]
        high, low = parts(small[...] + small_received[...])
        for k in range(groups):
            at = pl.ds(pl.multiple_of(jnp.bitwise_xor(where[2], k) * rows, rows), rows)
            value = tree([own[at]] + [r[at].astype(F32) for r in received])
            kind = outs[k].dtype
            outs[k][0:rows] = value.astype(kind)
            outs[k][rows : rows + extra] = high.astype(kind)
            outs[k][rows + extra :] = low.astype(kind)

    shape = (rows + 2 * extra, channels)
    return kernel_call(
        body,
        where,
        (own, small, small_received, *received),
        [jax.ShapeDtypeStruct(shape, BF16 if k else F32) for k in range(groups)],
        "split_dy",
    )


def add_dy(where, own, received, extra):
    rows = own.shape[0] - 2 * extra

    def add(own, received):
        big = tree([own[:rows]] + [r[:rows].astype(F32) for r in received])
        small = tree(
            [v[rows : rows + extra].astype(F32) + v[rows + extra :].astype(F32)
             for v in (own, *received)]
        )
        high, low = parts(small)
        return big.astype(BF16), high, low

    if rows % 16:
        return jnp.concatenate(add(own, received), axis=0)

    def body(where, own, *refs):
        big, high, low = add(own[...], [r[...] for r in refs[:-1]])
        refs[-1][0:rows] = big
        refs[-1][rows : rows + extra] = high
        refs[-1][rows + extra :] = low

    return kernel_call(
        body,
        where,
        (own, *received),
        jax.ShapeDtypeStruct(own.shape, BF16),
        "add_dy",
    )


def assemble(where, pieces, extra):
    peers = len(pieces)
    rows = pieces[0].shape[0] - 2 * extra
    channels = pieces[0].shape[1]

    def small_sum(values):
        return tree(
            [v[rows : rows + extra].astype(F32) + v[rows + extra :].astype(F32) for v in values]
        )

    if rows % 16:
        stacked = jnp.stack([p[:rows] for p in pieces])
        order = jnp.arange(peers, dtype=jnp.int32) ^ where[0]
        second = jnp.take(stacked, order, axis=0).reshape(peers * rows, channels)
        small = small_sum(pieces)
        return small[:10], small[10:12], second.astype(F32)

    def body(where, *refs):
        values, (first, gains, second) = refs[:peers], refs[peers:]
        small = small_sum([v[...] for v in values])
        first[...] = small[0:10]
        gains[...] = small[10:12]
        for k in range(peers):
            at = pl.ds(pl.multiple_of(jnp.bitwise_xor(where[0], k) * rows, rows), rows)
            second[at] = values[k][0:rows].astype(F32)

    return kernel_call(
        body,
        where,
        pieces,
        [
            jax.ShapeDtypeStruct((10, channels), F32),
            jax.ShapeDtypeStruct((2, channels), F32),
            jax.ShapeDtypeStruct((peers * rows, channels), F32),
        ],
        "assemble",
    )


def on_device(audio, counts, cotangent, conv_first, norm_gain, norm_bias, conv_second):
    peers = lax.axis_size("dx")
    members = lax.axis_size("dy")
    groups = members // 2
    own = lax.axis_index("dx")
    line = lax.axis_index("dy")
    where = jnp.stack([own, line % 2, line // 2]).astype(jnp.int32)
    crops, frames, channels = cotangent.shape[1:]
    slots = audio.shape[1]
    block = conv_second.shape[0] // members
    loss_scale = 1.0 / math.sqrt(peers * members * crops * frames)

    held = jnp.broadcast_to(counts.astype(BF16), (slots, 1))
    samples = audio.shape[2]
    packed = jnp.concatenate([audio[0], held], axis=1)
    packed = jnp.pad(packed, ((0, 0), (0, -(samples + 1) % LANES)))
    buffers = [packed] + [swap(packed, "dx", k) for k in range(1, peers)]

    taps = jnp.zeros((LANES, 2 * channels), BF16)
    taps = taps.at[0:10, :channels].set(conv_first).at[5:15, channels:].set(conv_first)
    gain = norm_gain.reshape(1, channels)
    bias = norm_bias.reshape(1, channels)

    keep, send, grad_rows, patches, stats = forward(
        where, buffers, cotangent[0], taps, conv_second, gain, bias, block, loss_scale
    )
    received = swap(send, "dy", 1)
    pieces = split_dx(where, keep, received, peers, block)
    received = [swap(pieces[k], "dx", k) for k in range(1, peers)]
    small = backward(grad_rows, patches, stats, taps, conv_second, gain, bias)
    small_received = swap(small, "dy", 1)
    pieces = split_dy(where, pieces[0], received, small, small_received, groups)
    received = [swap(pieces[k], "dy", 2 * k) for k in range(1, groups)]
    final = add_dy(where, pieces[0], received, small.shape[0])
    pieces = [final] + [swap(final, "dx", k) for k in range(1, peers)]
    return tuple(assemble(where, pieces, small.shape[0]))


def solution(mesh):
    in_specs = (P("dy", "dx", None), P("dy", "dx"), P("dy", "dx", None, None), P(), P(), P(), P())
    out_specs = (P(), P(), P("dy", None))
    return jax.shard_map(
        on_device, mesh=mesh, in_specs=in_specs, out_specs=out_specs, check_vma=False
    )
```

```python
import functools
import math

import jax
import jax.numpy as jnp
from jax import lax
from jax.experimental import pallas as pl
from jax.experimental.pallas import tpu as pltpu
from jax.sharding import PartitionSpec as P

BF16 = jnp.bfloat16
F32 = jnp.float32
LANES = 128
ROWS = 32
VMEM_SPEC = pl.BlockSpec(memory_space=pltpu.VMEM)
HBM_SPEC = pl.BlockSpec(memory_space=pltpu.HBM)
SMEM_SPEC = pl.BlockSpec(memory_space=pltpu.SMEM)


def gelu_cdf(value):
    return 0.5 * (1.0 + lax.erf(value * 0.7071067811865476))


def gelu_slope(value):
    return gelu_cdf(value) + value * jnp.exp(-0.5 * value * value) * 0.3989422804014327


def in_hbm(array):
    return pltpu.with_memory_space_constraint(array, pltpu.HBM)


def chunk(index, rows=ROWS):
    return pl.ds(pl.multiple_of(index * rows, rows), rows)


def fold(rows):
    total = rows[0:8]
    for start in range(8, rows.shape[0], 8):
        total = total + rows[start : start + 8]
    return total


def forward_kernel(
    peers, slots, crops, frames, channels, block, loss_scale, where, *refs
):
    buffers, refs = refs[:peers], refs[peers:]
    (taps, gain, bias, cot, second, keep, send, grad_rows, patches, stats) = refs[:10]
    (waves, wave_rows, even, odd, hid, rows, pre, acc) = refs[10:]
    crop = pl.program_id(0)
    samples = 10 * (frames + 1)
    first_len = 2 * frames + 1
    own = where[0]
    core = where[1]
    wanted = waves.shape[0]

    @pl.when(crop == 0)
    def _():
        counts = [buffer[0:1, samples : samples + 1].astype(F32) for buffer in buffers]
        slot = lax.broadcasted_iota(jnp.int32, (wanted, slots), 1)
        number = lax.broadcasted_iota(jnp.int32, (wanted, slots), 0) * peers + own
        picked = jnp.zeros(waves.shape, F32)
        for k in range(peers):
            holder = jnp.bitwise_xor(own, k)
            start = jnp.zeros((1, 1), F32)
            for other in range(peers):
                before = jnp.bitwise_xor(own, other) < holder
                start = start + jnp.where(before, counts[other], 0.0)
            first = jnp.broadcast_to(start.astype(jnp.int32), (wanted, slots))
            live = jnp.broadcast_to(counts[k].astype(jnp.int32), (wanted, slots))
            hit = (first + slot == number) & (slot < live)
            one_hot = jnp.where(hit, 1.0, 0.0).astype(BF16)
            picked = picked + jnp.dot(
                one_hot, buffers[k][...], preferred_element_type=F32
            )
        waves[...] = picked
        acc[...] = jnp.zeros_like(acc)

    period = 5 * LANES
    per_block = period // 10
    at = lax.broadcasted_iota(jnp.int32, (period, LANES), 0) % 10
    spread = jnp.where(
        at == lax.broadcasted_iota(jnp.int32, (period, LANES), 1), 1.0, 0.0
    ).astype(BF16)
    lane = lax.broadcasted_iota(jnp.int32, (per_block, period), 1)
    low = lax.broadcasted_iota(jnp.int32, (per_block, period), 0) * 10
    mask = (lane >= low) & (lane < low + 10)
    wave = waves[pl.ds(crop, 1), :]
    for part in range(10 * frames // period):
        piece = jnp.broadcast_to(
            wave[:, part * period : (part + 1) * period], (per_block, period)
        )
        piece = jnp.where(mask, piece, 0.0).astype(BF16)
        wave_rows[part * per_block : (part + 1) * per_block] = jnp.dot(
            piece, spread, preferred_element_type=F32
        )
    last = jnp.broadcast_to(wave[:, 10 * frames : 10 * frames + LANES], (16, LANES))
    last_row = lax.broadcasted_iota(jnp.int32, (16, LANES), 0)
    last_lane = lax.broadcasted_iota(jnp.int32, (16, LANES), 1)
    wave_rows[frames : frames + 16] = jnp.where((last_row == 0) & (last_lane < 10), last, 0.0)
    long = frames + 8
    both = wave_rows[0:long] + pltpu.roll(wave_rows[1 : long + 1], 10, 1)
    patch = both.astype(BF16)
    patches[crop] = patch

    first = jnp.dot(patch, taps[:, :channels], preferred_element_type=F32)
    even[...] = first
    total = fold(first)
    first = jnp.dot(patch[:frames], taps[:, channels:], preferred_element_type=F32)
    odd[...] = first
    total = total + fold(first)
    mean = jnp.sum(total, axis=0, keepdims=True) * (1.0 / first_len)
    tail_row = lax.broadcasted_iota(jnp.int32, (8, channels), 0) == 0

    def squares(i, total):
        a = even[chunk(i)] - mean
        b = odd[chunk(i)] - mean
        return total + fold(a * a + b * b)

    tail = even[frames:long] - mean
    total = lax.fori_loop(
        0, frames // ROWS, squares, jnp.where(tail_row, tail * tail, 0.0), unroll=True
    )
    var = jnp.sum(total, axis=0, keepdims=True) * (1.0 / first_len)
    inv_std = lax.rsqrt(var + 1e-05)
    stats[crop, 0:1] = mean
    stats[crop, 1:2] = inv_std
    scale = gain[...]
    shift = bias[...]

    def hidden(centre):
        value = centre * inv_std * scale + shift
        return value * gelu_cdf(value)

    def hide(i, carry):
        value = hidden(even[chunk(i)] - mean)
        hid[chunk(i)] = value
        rows[chunk(i), 0:channels] = value.astype(BF16)
        rows[chunk(i), channels : 2 * channels] = hidden(odd[chunk(i)] - mean).astype(BF16)
        return carry

    lax.fori_loop(0, frames // ROWS, hide, 0, unroll=True)
    hid[frames:long] = hidden(tail)
    rows[:, 2 * channels :] = hid[1 : frames + 1].astype(BF16)

    pre[...] = jnp.dot(rows[...], second[...], preferred_element_type=F32)

    def slope(i, carry):
        value = loss_scale * cot[crop, chunk(i)].astype(F32) * gelu_slope(pre[chunk(i)])
        grad_rows[crop, chunk(i)] = value.astype(BF16)
        return carry

    lax.fori_loop(0, frames // ROWS, slope, 0, unroll=True)
    acc[...] += lax.dot_general(
        rows[...],
        grad_rows[crop],
        (((0,), (0,)), ((), ())),
        preferred_element_type=F32,
    )

    @pl.when(crop == crops - 1)
    def _():
        for pair in range(acc.shape[0] // (2 * block)):
            mine = pl.ds(pl.multiple_of((2 * pair + core) * block, block), block)
            theirs = pl.ds(pl.multiple_of((2 * pair + 1 - core) * block, block), block)
            keep[pair * block : (pair + 1) * block] = acc[mine]
            send[pair * block : (pair + 1) * block] = acc[theirs].astype(BF16)


def forward(where, buffers, taps, gain, bias, cot, second, block, loss_scale):
    peers = len(buffers)
    slots, width = buffers[0].shape
    crops, frames, channels = cot.shape
    long = frames + 8
    half = second.shape[0] // 2
    return pl.pallas_call(
        functools.partial(
            forward_kernel, peers, slots, crops, frames, channels, block, loss_scale
        ),
        grid=(crops,),
        in_specs=[SMEM_SPEC] + [VMEM_SPEC] * (peers + 5),
        out_specs=[VMEM_SPEC] * 5,
        out_shape=[
            jax.ShapeDtypeStruct((half, channels), F32),
            jax.ShapeDtypeStruct((half, channels), BF16),
            jax.ShapeDtypeStruct((crops, frames, channels), BF16),
            jax.ShapeDtypeStruct((crops, long, LANES), BF16),
            jax.ShapeDtypeStruct((crops, 8, channels), F32),
        ],
        scratch_shapes=[
            pltpu.VMEM((max(8, crops), width), F32),
            pltpu.VMEM((frames + 16, LANES), F32),
            pltpu.VMEM((long, channels), F32),
            pltpu.VMEM((frames, channels), F32),
            pltpu.VMEM((long, channels), F32),
            pltpu.VMEM((frames, 3 * channels), BF16),
            pltpu.VMEM((frames, channels), F32),
            pltpu.VMEM(second.shape, F32),
        ],
        name="forward",
        compiler_params=pltpu.CompilerParams(vmem_limit_bytes=24 << 20),
    )(where, *buffers, taps, gain, bias, cot, second)


def prepare_kernel(channels, first, gain, bias, cot, second, *refs):
    taps, outs = refs[0], refs[1:5]
    early, wide, sems = refs[5:]
    copies = [
        pltpu.make_async_copy(source, target, sems.at[i])
        for i, (source, target) in enumerate(
            zip((first, gain, bias, cot, second), (early, *outs))
        )
    ]
    for copy in copies:
        copy.start()
    wide[...] = jnp.zeros_like(wide)
    copies[0].wait()
    weights = early[...].astype(F32)
    wide[0:10, :channels] = weights
    wide[5:15, channels:] = weights
    taps[0:16] = wide[...].astype(BF16)
    taps[16:] = jnp.zeros((LANES - 16, 2 * channels), BF16)
    for copy in copies[1:]:
        copy.wait()


def prepare(first, gain, bias, cot, second):
    channels = first.shape[1]
    shapes = [jax.ShapeDtypeStruct((LANES, 2 * channels), BF16)]
    shapes += [jax.ShapeDtypeStruct(a.shape, a.dtype) for a in (gain, bias, cot, second)]
    return pl.pallas_call(
        functools.partial(prepare_kernel, channels),
        in_specs=[HBM_SPEC] * 5,
        out_specs=[VMEM_SPEC] * 5,
        out_shape=shapes,
        scratch_shapes=[
            pltpu.VMEM(first.shape, BF16),
            pltpu.VMEM((16, 2 * channels), F32),
            pltpu.SemaphoreType.DMA((5,)),
        ],
        name="prepare",
        compiler_params=pltpu.CompilerParams(vmem_limit_bytes=8 << 20),
    )(*[in_hbm(a) for a in (first, gain, bias, cot, second)])


def backward_kernel(
    crops, frames, channels, grad_rows, patches, stats, taps, gain, bias, second,
    small, even, odd, cols, grad_even, grad_odd, late, first_acc, gains_acc,
):
    crop = pl.program_id(0)
    long = frames + 8
    first_len = 2 * frames + 1

    @pl.when(crop == 0)
    def _():
        first_acc[...] = jnp.zeros_like(first_acc)
        gains_acc[...] = jnp.zeros_like(gains_acc)

    patch = patches[crop]
    even[...] = jnp.dot(patch, taps[:, :channels], preferred_element_type=F32)
    odd[...] = jnp.dot(patch[:frames], taps[:, channels:], preferred_element_type=F32)
    cols[...] = lax.dot_general(
        grad_rows[crop],
        second[: 2 * channels],
        (((1,), (1,)), ((), ())),
        preferred_element_type=F32,
    )
    late[0:8] = jnp.zeros((8, channels), F32)
    late[8 : frames + 8] = lax.dot_general(
        grad_rows[crop],
        second[2 * channels :],
        (((1,), (1,)), ((), ())),
        preferred_element_type=F32,
    )
    mean = stats[crop, 0:1]
    inv_std = stats[crop, 1:2]
    scale = gain[...]
    shift = bias[...]

    def shift_grad(pre_norm, grad_hidden):
        normed = (pre_norm - mean) * inv_std
        grad = grad_hidden * gelu_slope(normed * scale + shift)
        return normed, grad

    def first_pass(i, carry):
        shifts, gains = carry
        normed, grad = shift_grad(
            even[chunk(i)], cols[chunk(i), 0:channels] + late[pl.ds(i * ROWS + 7, ROWS), :]
        )
        even[chunk(i)] = normed
        grad_even[chunk(i)] = grad
        shifts = shifts + fold(grad)
        gains = gains + fold(grad * normed)
        normed, grad = shift_grad(odd[chunk(i)], cols[chunk(i), channels:])
        odd[chunk(i)] = normed
        grad_odd[chunk(i)] = grad
        return shifts + fold(grad), gains + fold(grad * normed)

    tail_row = lax.broadcasted_iota(jnp.int32, (8, channels), 0) == 0
    tail_normed, tail_grad = shift_grad(
        even[frames:long],
        jnp.broadcast_to(late[frames + 7 : frames + 8], (8, channels)),
    )
    tail_grad = jnp.where(tail_row, tail_grad, 0.0)
    carry = (tail_grad, tail_grad * tail_normed)
    for i in range(frames // ROWS):
        carry = first_pass(i, carry)
    shifts = jnp.sum(carry[0], axis=0, keepdims=True)
    gains = jnp.sum(carry[1], axis=0, keepdims=True)
    gains_acc[0:1] += gains
    gains_acc[1:2] += shifts
    shifts = shifts * (1.0 / first_len)
    gains = gains * (1.0 / first_len)
    outer = inv_std * scale

    def grad_pre(grad, normed):
        return (outer * (grad - shifts - normed * gains)).astype(BF16)

    tail_pre = jnp.where(tail_row, outer * (tail_grad - shifts - tail_normed * gains), 0.0)
    grads = [grad_pre(grad_even[chunk(i)], even[chunk(i)]) for i in range(frames // ROWS)]
    whole_even = jnp.concatenate(grads, axis=0)
    grads = [grad_pre(grad_odd[chunk(i)], odd[chunk(i)]) for i in range(frames // ROWS)]
    whole_odd = jnp.concatenate(grads, axis=0)

    def outer_sum(a, b):
        return lax.dot_general(a, b, (((0,), (0,)), ((), ())), preferred_element_type=F32)

    first_acc[0:LANES] += outer_sum(patch[:frames], whole_even) + outer_sum(
        patch[frames:long], tail_pre.astype(BF16)
    )
    first_acc[LANES:] += outer_sum(patch[:frames], whole_odd)

    @pl.when(crop == crops - 1)
    def _():
        small[...] = jnp.zeros_like(small)
        small[0:10] = first_acc[0:10] + first_acc[LANES + 5 : LANES + 15]
        small[10:12] = gains_acc[0:2]


def backward(grad_rows, patches, stats, taps, gain, bias, second):
    crops, frames, channels = grad_rows.shape
    long = frames + 8
    return pl.pallas_call(
        functools.partial(backward_kernel, crops, frames, channels),
        grid=(crops,),
        in_specs=[VMEM_SPEC] * 7,
        out_specs=VMEM_SPEC,
        out_shape=jax.ShapeDtypeStruct((16, channels), F32),
        scratch_shapes=[
            pltpu.VMEM((long, channels), F32),
            pltpu.VMEM((frames, channels), F32),
            pltpu.VMEM((frames, 2 * channels), F32),
            pltpu.VMEM((frames, channels), F32),
            pltpu.VMEM((frames, channels), F32),
            pltpu.VMEM((long, channels), F32),
            pltpu.VMEM((2 * LANES, channels), F32),
            pltpu.VMEM((8, channels), F32),
        ],
        name="backward",
        compiler_params=pltpu.CompilerParams(vmem_limit_bytes=16 << 20),
    )(grad_rows, patches, stats, taps, gain, bias, second)


def tree(values):
    while len(values) > 1:
        values = [values[i] + values[i + 1] for i in range(0, len(values), 2)]
    return values[0]


def swap(value, axis, key):
    return lax.ppermute(value, axis, [(i, i ^ key) for i in range(lax.axis_size(axis))])


def parts(value):
    high = value.astype(BF16)
    low = (value - high.astype(F32)).astype(BF16)
    return high, low


def kernel_call(kernel, where, arrays, out_shape, name):
    return pl.pallas_call(
        kernel,
        in_specs=[SMEM_SPEC] + [VMEM_SPEC] * len(arrays),
        out_specs=jax.tree.map(lambda _: VMEM_SPEC, out_shape),
        out_shape=out_shape,
        name=name,
        compiler_params=pltpu.CompilerParams(vmem_limit_bytes=4 << 20),
    )(where, *arrays)


def split_dx(where, keep, received, peers, block):
    half, channels = keep.shape
    groups = half // block
    rows = block // peers
    if rows % 16:
        total = (keep + received.astype(F32)).reshape(groups, peers, rows, channels)
        picked = [
            lax.dynamic_index_in_dim(total, where[0] ^ k, axis=1, keepdims=False)
            for k in range(peers)
        ]
        picked = [p.reshape(groups * rows, channels) for p in picked]
        return [picked[0]] + [p.astype(BF16) for p in picked[1:]]

    def body(where, keep, received, *outs):
        for k in range(peers):
            part = jnp.bitwise_xor(where[0], k)
            for g in range(groups):
                at = pl.ds(pl.multiple_of(g * block + part * rows, rows), rows)
                value = keep[at] + received[at].astype(F32)
                outs[k][g * rows : (g + 1) * rows] = value.astype(outs[k].dtype)

    shape = (groups * rows, channels)
    return kernel_call(
        body,
        where,
        (keep, received),
        [jax.ShapeDtypeStruct(shape, BF16 if k else F32) for k in range(peers)],
        "split_dx",
    )


def split_dy(where, own, received, small, small_received, groups):
    rows = own.shape[0] // groups
    channels = own.shape[1]
    extra = small.shape[0]
    if rows % 16:
        total = tree([own] + [r.astype(F32) for r in received])
        total = total.reshape(groups, rows, channels)
        high, low = parts(small + small_received)
        picked = [
            lax.dynamic_index_in_dim(total, where[2] ^ k, axis=0, keepdims=False)
            for k in range(groups)
        ]
        first = jnp.concatenate([picked[0], high.astype(F32), low.astype(F32)], axis=0)
        return [first] + [
            jnp.concatenate([p.astype(BF16), high, low], axis=0) for p in picked[1:]
        ]

    def body(where, own, small, small_received, *refs):
        received, outs = refs[: len(refs) - groups], refs[len(refs) - groups :]
        high, low = parts(small[...] + small_received[...])
        for k in range(groups):
            at = pl.ds(pl.multiple_of(jnp.bitwise_xor(where[2], k) * rows, rows), rows)
            value = tree([own[at]] + [r[at].astype(F32) for r in received])
            kind = outs[k].dtype
            outs[k][0:rows] = value.astype(kind)
            outs[k][rows : rows + extra] = high.astype(kind)
            outs[k][rows + extra :] = low.astype(kind)

    shape = (rows + 2 * extra, channels)
    return kernel_call(
        body,
        where,
        (own, small, small_received, *received),
        [jax.ShapeDtypeStruct(shape, BF16 if k else F32) for k in range(groups)],
        "split_dy",
    )


def add_dy(where, own, received, extra):
    rows = own.shape[0] - 2 * extra

    def add(own, received):
        big = tree([own[:rows]] + [r[:rows].astype(F32) for r in received])
        small = tree(
            [v[rows : rows + extra].astype(F32) + v[rows + extra :].astype(F32)
             for v in (own, *received)]
        )
        high, low = parts(small)
        return big.astype(BF16), high, low

    if rows % 16:
        return jnp.concatenate(add(own, received), axis=0)

    def body(where, own, *refs):
        big, high, low = add(own[...], [r[...] for r in refs[:-1]])
        refs[-1][0:rows] = big
        refs[-1][rows : rows + extra] = high
        refs[-1][rows + extra :] = low

    return kernel_call(
        body,
        where,
        (own, *received),
        jax.ShapeDtypeStruct(own.shape, BF16),
        "add_dy",
    )


def assemble(where, pieces, extra):
    peers = len(pieces)
    rows = pieces[0].shape[0] - 2 * extra
    channels = pieces[0].shape[1]

    def small_sum(values):
        return tree(
            [v[rows : rows + extra].astype(F32) + v[rows + extra :].astype(F32) for v in values]
        )

    if rows % 16:
        stacked = jnp.stack([p[:rows] for p in pieces])
        order = jnp.arange(peers, dtype=jnp.int32) ^ where[0]
        second = jnp.take(stacked, order, axis=0).reshape(peers * rows, channels)
        small = small_sum(pieces)
        return small[:10], small[10:12], second.astype(F32)

    def body(where, *refs):
        values, (first, gains, second) = refs[:peers], refs[peers:]
        small = small_sum([v[...] for v in values])
        first[...] = small[0:10]
        gains[...] = small[10:12]
        for k in range(peers):
            at = pl.ds(pl.multiple_of(jnp.bitwise_xor(where[0], k) * rows, rows), rows)
            second[at] = values[k][0:rows].astype(F32)

    return kernel_call(
        body,
        where,
        pieces,
        [
            jax.ShapeDtypeStruct((10, channels), F32),
            jax.ShapeDtypeStruct((2, channels), F32),
            jax.ShapeDtypeStruct((peers * rows, channels), F32),
        ],
        "assemble",
    )


def on_device(audio, counts, cotangent, conv_first, norm_gain, norm_bias, conv_second):
    peers = lax.axis_size("dx")
    members = lax.axis_size("dy")
    groups = members // 2
    own = lax.axis_index("dx")
    line = lax.axis_index("dy")
    where = jnp.stack([own, line % 2, line // 2]).astype(jnp.int32)
    crops, frames, channels = cotangent.shape[1:]
    slots = audio.shape[1]
    block = conv_second.shape[0] // members
    loss_scale = 1.0 / math.sqrt(peers * members * crops * frames)

    samples = audio.shape[2]
    held = jnp.broadcast_to(counts.astype(BF16), (slots, 1))
    packed = jnp.concatenate([audio[0], held], axis=1)
    packed = jnp.pad(packed, ((0, 0), (0, -(samples + 1) % LANES)))
    buffers = [packed] + [swap(packed, "dx", k) for k in range(1, peers)]
    taps, gain, bias, cot, second = prepare(
        conv_first,
        norm_gain.reshape(1, channels),
        norm_bias.reshape(1, channels),
        cotangent[0],
        conv_second,
    )
    keep, send, grad_rows, patches, stats = forward(
        where, buffers, taps, gain, bias, cot, second, block, loss_scale
    )
    received = swap(send, "dy", 1)
    pieces = split_dx(where, keep, received, peers, block)
    received = [swap(pieces[k], "dx", k) for k in range(1, peers)]
    small = backward(grad_rows, patches, stats, taps, gain, bias, second)
    small_received = swap(small, "dy", 1)
    pieces = split_dy(where, pieces[0], received, small, small_received, groups)
    received = [swap(pieces[k], "dy", 2 * k) for k in range(1, groups)]
    final = add_dy(where, pieces[0], received, small.shape[0])
    pieces = [final] + [swap(final, "dx", k) for k in range(1, peers)]
    return tuple(assemble(where, pieces, small.shape[0]))


def solution(mesh):
    in_specs = (P("dy", "dx", None), P("dy", "dx"), P("dy", "dx", None, None), P(), P(), P(), P())
    out_specs = (P(), P(), P("dy", None))
    return jax.shard_map(
        on_device, mesh=mesh, in_specs=in_specs, out_specs=out_specs, check_vma=False
    )
```

```python
import functools
import math

import jax
import jax.numpy as jnp
from jax import lax
from jax.experimental import pallas as pl
from jax.experimental.pallas import tpu as pltpu
from jax.sharding import PartitionSpec as P

BF16 = jnp.bfloat16
F32 = jnp.float32
LANES = 128
HALF_ROOT = 0.7071067811865476
ROWS = 32
VMEM_SPEC = pl.BlockSpec(memory_space=pltpu.VMEM)
HBM_SPEC = pl.BlockSpec(memory_space=pltpu.HBM)
SMEM_SPEC = pl.BlockSpec(memory_space=pltpu.SMEM)


def gelu_cdf(value):
    return 0.5 * (1.0 + lax.erf(value * 0.7071067811865476))


def gelu_slope(value):
    return gelu_cdf(value) + value * jnp.exp(-0.5 * value * value) * 0.3989422804014327


def in_hbm(array):
    return pltpu.with_memory_space_constraint(array, pltpu.HBM)


def rows_of(index):
    return slice(index * ROWS, (index + 1) * ROWS)


def chunk(index, rows=ROWS):
    return pl.ds(pl.multiple_of(index * rows, rows), rows)


def fold(rows):
    total = rows[0:8]
    for start in range(8, rows.shape[0], 8):
        total = total + rows[start : start + 8]
    return total


def forward_kernel(peers, slots, crops, frames, channels, block, loss_scale, where, *refs):
    buffers, refs = refs[:peers], refs[peers:]
    (taps, gain, bias, spread, mask, cot, second) = refs[:7]
    (keep, send, grad_rows, patches, stats) = refs[7:12]
    (waves, acc), refs = refs[12:14], refs[14:]
    samples = 10 * (frames + 1)
    first_len = 2 * frames + 1
    long = frames + 8
    period = spread.shape[0]
    per_block = period // 10
    own = where[0]
    core = where[1]
    wanted = waves.shape[0]

    counts = [buffer[0:1, samples : samples + 1].astype(F32) for buffer in buffers]
    slot = lax.broadcasted_iota(jnp.int32, (wanted, slots), 1)
    number = lax.broadcasted_iota(jnp.int32, (wanted, slots), 0) * peers + own
    picked = jnp.zeros(waves.shape, F32)
    for k in range(peers):
        holder = jnp.bitwise_xor(own, k)
        start = jnp.zeros((1, 1), F32)
        for other in range(peers):
            before = jnp.bitwise_xor(own, other) < holder
            start = start + jnp.where(before, counts[other], 0.0)
        first = jnp.broadcast_to(start.astype(jnp.int32), (wanted, slots))
        live = jnp.broadcast_to(counts[k].astype(jnp.int32), (wanted, slots))
        hit = (first + slot == number) & (slot < live)
        one_hot = jnp.where(hit, 1.0, 0.0).astype(BF16)
        picked = picked + jnp.dot(one_hot, buffers[k][...], preferred_element_type=F32)
    waves[...] = picked
    last_row = lax.broadcasted_iota(jnp.int32, (16, LANES), 0)
    last_lane = lax.broadcasted_iota(jnp.int32, (16, LANES), 1)
    last_mask = (last_row == 0) & (last_lane < 10)
    tail_row = lax.broadcasted_iota(jnp.int32, (8, channels), 0) == 0
    steps = range(frames // ROWS)

    def scratch(crop):
        return refs[6 * (crop % 2) : 6 * (crop % 2) + 6]

    def frontend(crop):
        wave_rows, even, odd, hid, rows, _ = scratch(crop)
        wave = waves[crop : crop + 1]
        pieces = []
        for part in range(10 * frames // period):
            piece = jnp.broadcast_to(wave[:, part * period : (part + 1) * period], (16, period))
            piece = jnp.concatenate([piece.astype(BF16)] * (per_block // 16), axis=0)
            pieces.append(piece * mask[...])
        wave_rows[0:frames] = jnp.dot(
            jnp.concatenate(pieces, axis=0), spread[...], preferred_element_type=F32
        )
        last = jnp.broadcast_to(wave[:, 10 * frames : 10 * frames + LANES], (16, LANES))
        wave_rows[frames : frames + 16] = jnp.where(last_mask, last, 0.0)
        both = wave_rows[0:long] + pltpu.roll(wave_rows[1 : long + 1], 10, 1)
        patch = both.astype(BF16)
        patches[crop] = patch

        first = jnp.dot(patch, taps[:, :channels], preferred_element_type=F32)
        even[...] = first
        total = fold(first)
        first = jnp.dot(patch[:frames], taps[:, channels:], preferred_element_type=F32)
        odd[...] = first
        total = total + fold(first)
        mean = jnp.sum(total, axis=0, keepdims=True) * (1.0 / first_len)
        tail = even[frames:long] - mean
        total = jnp.where(tail_row, tail * tail, 0.0)
        for i in steps:
            a = even[rows_of(i)] - mean
            b = odd[rows_of(i)] - mean
            total = total + fold(a * a + b * b)
        var = jnp.sum(total, axis=0, keepdims=True) * (1.0 / first_len)
        inv_std = lax.rsqrt(var + 1e-05)
        stats[crop, 0:1] = mean
        stats[crop, 1:2] = inv_std
        scale = inv_std * gain[...] * HALF_ROOT
        shift = bias[...] * HALF_ROOT

        def hidden(centre):
            value = centre * scale + shift
            return (value * HALF_ROOT) * (1.0 + lax.erf(value))

        for i in steps:
            value = hidden(even[rows_of(i)] - mean)
            hid[rows_of(i)] = value
            rows[rows_of(i), 0:channels] = value.astype(BF16)
            value = hidden(odd[rows_of(i)] - mean)
            rows[rows_of(i), channels : 2 * channels] = value.astype(BF16)
        hid[frames:long] = hidden(tail)
        for i in steps:
            value = hid[i * ROWS + 1 : (i + 1) * ROWS + 1]
            rows[rows_of(i), 2 * channels :] = value.astype(BF16)

    def middle(crop):
        rows, pre = scratch(crop)[4:6]
        pre[...] = jnp.dot(rows[...], second[...], preferred_element_type=F32)
        for i in steps:
            value = pre[rows_of(i)]
            scaled = value * HALF_ROOT
            bell = jnp.exp2((scaled * scaled) * (-1.4426950408889634))
            slope = (1.0 + lax.erf(scaled)) * (0.5 * loss_scale) + (value * bell) * (
                0.3989422804014327 * loss_scale
            )
            value = cot[crop, rows_of(i)].astype(F32) * slope
            grad_rows[crop, rows_of(i)] = value.astype(BF16)

    def outer(crop):
        rows = scratch(crop)[4]
        product = lax.dot_general(
            rows[...],
            grad_rows[crop],
            (((0,), (0,)), ((), ())),
            preferred_element_type=F32,
        )
        acc[...] = acc[...] + product if crop else product

    frontend(0)
    for crop in range(crops):
        middle(crop)
        if crop + 1 < crops:
            frontend(crop + 1)
        outer(crop)
    for pair in range(acc.shape[0] // (2 * block)):
        mine = pl.ds(pl.multiple_of((2 * pair + core) * block, block), block)
        theirs = pl.ds(pl.multiple_of((2 * pair + 1 - core) * block, block), block)
        keep[pair * block : (pair + 1) * block] = acc[mine]
        send[pair * block : (pair + 1) * block] = acc[theirs].astype(BF16)


def forward(where, buffers, taps, gain, bias, spread, mask, cot, second, block, loss_scale):
    peers = len(buffers)
    slots, width = buffers[0].shape
    crops, frames, channels = cot.shape
    long = frames + 8
    half = second.shape[0] // 2
    per_crop = [
        pltpu.VMEM((frames + 16, LANES), F32),
        pltpu.VMEM((long, channels), F32),
        pltpu.VMEM((frames, channels), F32),
        pltpu.VMEM((long, channels), F32),
        pltpu.VMEM((frames, 3 * channels), BF16),
        pltpu.VMEM((frames, channels), F32),
    ]
    return pl.pallas_call(
        functools.partial(
            forward_kernel, peers, slots, crops, frames, channels, block, loss_scale
        ),
        in_specs=[SMEM_SPEC] + [VMEM_SPEC] * (peers + 7),
        out_specs=[VMEM_SPEC] * 5,
        out_shape=[
            jax.ShapeDtypeStruct((half, channels), F32),
            jax.ShapeDtypeStruct((half, channels), BF16),
            jax.ShapeDtypeStruct((crops, frames, channels), BF16),
            jax.ShapeDtypeStruct((crops, long, LANES), BF16),
            jax.ShapeDtypeStruct((crops, 8, channels), F32),
        ],
        scratch_shapes=[
            pltpu.VMEM((max(8, crops), width), F32),
            pltpu.VMEM(second.shape, F32),
            *per_crop,
            *per_crop,
        ],
        name="forward",
        compiler_params=pltpu.CompilerParams(vmem_limit_bytes=24 << 20),
    )(where, *buffers, taps, gain, bias, spread, mask, cot, second)


def prepare_kernel(channels, first, gain, bias, cot, second, *refs):
    (taps, spread, mask), outs = refs[:3], refs[3:7]
    early, wide, sems = refs[7:]
    copies = [
        pltpu.make_async_copy(source, target, sems.at[i])
        for i, (source, target) in enumerate(
            zip((first, gain, bias, cot, second), (early, *outs))
        )
    ]
    for copy in copies:
        copy.start()
    at = lax.broadcasted_iota(jnp.int32, spread.shape, 0) % 10
    hit = at == lax.broadcasted_iota(jnp.int32, spread.shape, 1)
    spread[...] = jnp.where(hit, 1.0, 0.0).astype(BF16)
    lane = lax.broadcasted_iota(jnp.int32, mask.shape, 1)
    low = lax.broadcasted_iota(jnp.int32, mask.shape, 0) * 10
    hit = (lane >= low) & (lane < low + 10)
    mask[...] = jnp.where(hit, 1.0, 0.0).astype(BF16)
    wide[...] = jnp.zeros_like(wide)
    copies[0].wait()
    weights = early[...].astype(F32)
    wide[0:10, :channels] = weights
    wide[5:15, channels:] = weights
    taps[0:16] = wide[...].astype(BF16)
    taps[16:] = jnp.zeros((LANES - 16, 2 * channels), BF16)
    for copy in copies[1:]:
        copy.wait()


def prepare(first, gain, bias, cot, second):
    channels = first.shape[1]
    period = 5 * LANES
    shapes = [
        jax.ShapeDtypeStruct((LANES, 2 * channels), BF16),
        jax.ShapeDtypeStruct((period, LANES), BF16),
        jax.ShapeDtypeStruct((period // 10, period), BF16),
    ]
    shapes += [jax.ShapeDtypeStruct(a.shape, a.dtype) for a in (gain, bias, cot, second)]
    return pl.pallas_call(
        functools.partial(prepare_kernel, channels),
        in_specs=[HBM_SPEC] * 5,
        out_specs=[VMEM_SPEC] * 7,
        out_shape=shapes,
        scratch_shapes=[
            pltpu.VMEM(first.shape, BF16),
            pltpu.VMEM((16, 2 * channels), F32),
            pltpu.SemaphoreType.DMA((5,)),
        ],
        name="prepare",
        compiler_params=pltpu.CompilerParams(vmem_limit_bytes=8 << 20),
    )(*[in_hbm(a) for a in (first, gain, bias, cot, second)])


def backward_kernel(
    crops, frames, channels, grad_rows, patches, stats, taps, gain, bias, second,
    small, even, odd, cols, grad_even, grad_odd, late, first_acc, gains_acc,
):
    crop = pl.program_id(0)
    long = frames + 8
    first_len = 2 * frames + 1

    @pl.when(crop == 0)
    def _():
        first_acc[...] = jnp.zeros_like(first_acc)
        gains_acc[...] = jnp.zeros_like(gains_acc)

    patch = patches[crop]
    even[...] = jnp.dot(patch, taps[:, :channels], preferred_element_type=F32)
    odd[...] = jnp.dot(patch[:frames], taps[:, channels:], preferred_element_type=F32)
    cols[...] = lax.dot_general(
        grad_rows[crop],
        second[: 2 * channels],
        (((1,), (1,)), ((), ())),
        preferred_element_type=F32,
    )
    late[0:8] = jnp.zeros((8, channels), F32)
    late[8 : frames + 8] = lax.dot_general(
        grad_rows[crop],
        second[2 * channels :],
        (((1,), (1,)), ((), ())),
        preferred_element_type=F32,
    )
    mean = stats[crop, 0:1]
    inv_std = stats[crop, 1:2]
    scale = gain[...]
    shift = bias[...]

    def shift_grad(pre_norm, grad_hidden):
        normed = (pre_norm - mean) * inv_std
        grad = grad_hidden * gelu_slope(normed * scale + shift)
        return normed, grad

    def first_pass(i, carry):
        shifts, gains = carry
        normed, grad = shift_grad(
            even[chunk(i)], cols[chunk(i), 0:channels] + late[pl.ds(i * ROWS + 7, ROWS), :]
        )
        even[chunk(i)] = normed
        grad_even[chunk(i)] = grad
        shifts = shifts + fold(grad)
        gains = gains + fold(grad * normed)
        normed, grad = shift_grad(odd[chunk(i)], cols[chunk(i), channels:])
        odd[chunk(i)] = normed
        grad_odd[chunk(i)] = grad
        return shifts + fold(grad), gains + fold(grad * normed)

    tail_row = lax.broadcasted_iota(jnp.int32, (8, channels), 0) == 0
    tail_normed, tail_grad = shift_grad(
        even[frames:long],
        jnp.broadcast_to(late[frames + 7 : frames + 8], (8, channels)),
    )
    tail_grad = jnp.where(tail_row, tail_grad, 0.0)
    carry = (tail_grad, tail_grad * tail_normed)
    for i in range(frames // ROWS):
        carry = first_pass(i, carry)
    shifts = jnp.sum(carry[0], axis=0, keepdims=True)
    gains = jnp.sum(carry[1], axis=0, keepdims=True)
    gains_acc[0:1] += gains
    gains_acc[1:2] += shifts
    shifts = shifts * (1.0 / first_len)
    gains = gains * (1.0 / first_len)
    outer = inv_std * scale

    def grad_pre(grad, normed):
        return (outer * (grad - shifts - normed * gains)).astype(BF16)

    tail_pre = jnp.where(tail_row, outer * (tail_grad - shifts - tail_normed * gains), 0.0)
    grads = [grad_pre(grad_even[chunk(i)], even[chunk(i)]) for i in range(frames // ROWS)]
    whole_even = jnp.concatenate(grads, axis=0)
    grads = [grad_pre(grad_odd[chunk(i)], odd[chunk(i)]) for i in range(frames // ROWS)]
    whole_odd = jnp.concatenate(grads, axis=0)

    def outer_sum(a, b):
        return lax.dot_general(a, b, (((0,), (0,)), ((), ())), preferred_element_type=F32)

    first_acc[0:LANES] += outer_sum(patch[:frames], whole_even) + outer_sum(
        patch[frames:long], tail_pre.astype(BF16)
    )
    first_acc[LANES:] += outer_sum(patch[:frames], whole_odd)

    @pl.when(crop == crops - 1)
    def _():
        small[...] = jnp.zeros_like(small)
        small[0:10] = first_acc[0:10] + first_acc[LANES + 5 : LANES + 15]
        small[10:12] = gains_acc[0:2]


def backward(grad_rows, patches, stats, taps, gain, bias, second):
    crops, frames, channels = grad_rows.shape
    long = frames + 8
    return pl.pallas_call(
        functools.partial(backward_kernel, crops, frames, channels),
        grid=(crops,),
        in_specs=[VMEM_SPEC] * 7,
        out_specs=VMEM_SPEC,
        out_shape=jax.ShapeDtypeStruct((16, channels), F32),
        scratch_shapes=[
            pltpu.VMEM((long, channels), F32),
            pltpu.VMEM((frames, channels), F32),
            pltpu.VMEM((frames, 2 * channels), F32),
            pltpu.VMEM((frames, channels), F32),
            pltpu.VMEM((frames, channels), F32),
            pltpu.VMEM((long, channels), F32),
            pltpu.VMEM((2 * LANES, channels), F32),
            pltpu.VMEM((8, channels), F32),
        ],
        name="backward",
        compiler_params=pltpu.CompilerParams(vmem_limit_bytes=16 << 20),
    )(grad_rows, patches, stats, taps, gain, bias, second)


def tree(values):
    while len(values) > 1:
        values = [values[i] + values[i + 1] for i in range(0, len(values), 2)]
    return values[0]


def swap(value, axis, key):
    return lax.ppermute(value, axis, [(i, i ^ key) for i in range(lax.axis_size(axis))])


def parts(value):
    high = value.astype(BF16)
    low = (value - high.astype(F32)).astype(BF16)
    return high, low


def kernel_call(kernel, where, arrays, out_shape, name):
    return pl.pallas_call(
        kernel,
        in_specs=[SMEM_SPEC] + [VMEM_SPEC] * len(arrays),
        out_specs=jax.tree.map(lambda _: VMEM_SPEC, out_shape),
        out_shape=out_shape,
        name=name,
        compiler_params=pltpu.CompilerParams(vmem_limit_bytes=4 << 20),
    )(where, *arrays)


def split_dx(where, keep, received, peers, block):
    half, channels = keep.shape
    groups = half // block
    rows = block // peers
    if rows % 16:
        total = (keep + received.astype(F32)).reshape(groups, peers, rows, channels)
        picked = [
            lax.dynamic_index_in_dim(total, where[0] ^ k, axis=1, keepdims=False)
            for k in range(peers)
        ]
        picked = [p.reshape(groups * rows, channels) for p in picked]
        return [picked[0]] + [p.astype(BF16) for p in picked[1:]]

    def body(where, keep, received, *outs):
        for k in range(peers):
            part = jnp.bitwise_xor(where[0], k)
            for g in range(groups):
                at = pl.ds(pl.multiple_of(g * block + part * rows, rows), rows)
                value = keep[at] + received[at].astype(F32)
                outs[k][g * rows : (g + 1) * rows] = value.astype(outs[k].dtype)

    shape = (groups * rows, channels)
    return kernel_call(
        body,
        where,
        (keep, received),
        [jax.ShapeDtypeStruct(shape, BF16 if k else F32) for k in range(peers)],
        "split_dx",
    )


def split_dy(where, own, received, small, small_received, groups):
    rows = own.shape[0] // groups
    channels = own.shape[1]
    extra = small.shape[0]
    if rows % 16:
        total = tree([own] + [r.astype(F32) for r in received])
        total = total.reshape(groups, rows, channels)
        high, low = parts(small + small_received)
        picked = [
            lax.dynamic_index_in_dim(total, where[2] ^ k, axis=0, keepdims=False)
            for k in range(groups)
        ]
        first = jnp.concatenate([picked[0], high.astype(F32), low.astype(F32)], axis=0)
        return [first] + [
            jnp.concatenate([p.astype(BF16), high, low], axis=0) for p in picked[1:]
        ]

    def body(where, own, small, small_received, *refs):
        received, outs = refs[: len(refs) - groups], refs[len(refs) - groups :]
        high, low = parts(small[...] + small_received[...])
        for k in range(groups):
            at = pl.ds(pl.multiple_of(jnp.bitwise_xor(where[2], k) * rows, rows), rows)
            value = tree([own[at]] + [r[at].astype(F32) for r in received])
            kind = outs[k].dtype
            outs[k][0:rows] = value.astype(kind)
            outs[k][rows : rows + extra] = high.astype(kind)
            outs[k][rows + extra :] = low.astype(kind)

    shape = (rows + 2 * extra, channels)
    return kernel_call(
        body,
        where,
        (own, small, small_received, *received),
        [jax.ShapeDtypeStruct(shape, BF16 if k else F32) for k in range(groups)],
        "split_dy",
    )


def add_dy(where, own, received, extra):
    rows = own.shape[0] - 2 * extra

    def add(own, received):
        big = tree([own[:rows]] + [r[:rows].astype(F32) for r in received])
        small = tree(
            [v[rows : rows + extra].astype(F32) + v[rows + extra :].astype(F32)
             for v in (own, *received)]
        )
        high, low = parts(small)
        return big.astype(BF16), high, low

    if rows % 16:
        return jnp.concatenate(add(own, received), axis=0)

    def body(where, own, *refs):
        big, high, low = add(own[...], [r[...] for r in refs[:-1]])
        refs[-1][0:rows] = big
        refs[-1][rows : rows + extra] = high
        refs[-1][rows + extra :] = low

    return kernel_call(
        body,
        where,
        (own, *received),
        jax.ShapeDtypeStruct(own.shape, BF16),
        "add_dy",
    )


def assemble(where, pieces, extra):
    peers = len(pieces)
    rows = pieces[0].shape[0] - 2 * extra
    channels = pieces[0].shape[1]

    def small_sum(values):
        return tree(
            [v[rows : rows + extra].astype(F32) + v[rows + extra :].astype(F32) for v in values]
        )

    if rows % 16:
        stacked = jnp.stack([p[:rows] for p in pieces])
        order = jnp.arange(peers, dtype=jnp.int32) ^ where[0]
        second = jnp.take(stacked, order, axis=0).reshape(peers * rows, channels)
        small = small_sum(pieces)
        return small[:10], small[10:12], second.astype(F32)

    def body(where, *refs):
        values, (first, gains, second) = refs[:peers], refs[peers:]
        small = small_sum([v[...] for v in values])
        first[...] = small[0:10]
        gains[...] = small[10:12]
        for k in range(peers):
            at = pl.ds(pl.multiple_of(jnp.bitwise_xor(where[0], k) * rows, rows), rows)
            second[at] = values[k][0:rows].astype(F32)

    return kernel_call(
        body,
        where,
        pieces,
        [
            jax.ShapeDtypeStruct((10, channels), F32),
            jax.ShapeDtypeStruct((2, channels), F32),
            jax.ShapeDtypeStruct((peers * rows, channels), F32),
        ],
        "assemble",
    )


def on_device(audio, counts, cotangent, conv_first, norm_gain, norm_bias, conv_second):
    peers = lax.axis_size("dx")
    members = lax.axis_size("dy")
    groups = members // 2
    own = lax.axis_index("dx")
    line = lax.axis_index("dy")
    where = jnp.stack([own, line % 2, line // 2]).astype(jnp.int32)
    crops, frames, channels = cotangent.shape[1:]
    slots = audio.shape[1]
    block = conv_second.shape[0] // members
    loss_scale = 1.0 / math.sqrt(peers * members * crops * frames)

    samples = audio.shape[2]
    held = jnp.broadcast_to(counts.astype(BF16), (slots, 1))
    packed = jnp.concatenate([audio[0], held], axis=1)
    packed = jnp.pad(packed, ((0, 0), (0, -(samples + 1) % LANES)))
    buffers = [packed] + [swap(packed, "dx", k) for k in range(1, peers)]
    taps, spread, mask, gain, bias, cot, second = prepare(
        conv_first,
        norm_gain.reshape(1, channels),
        norm_bias.reshape(1, channels),
        cotangent[0],
        conv_second,
    )
    keep, send, grad_rows, patches, stats = forward(
        where, buffers, taps, gain, bias, spread, mask, cot, second, block, loss_scale
    )
    received = swap(send, "dy", 1)
    pieces = split_dx(where, keep, received, peers, block)
    received = [swap(pieces[k], "dx", k) for k in range(1, peers)]
    small = backward(grad_rows, patches, stats, taps, gain, bias, second)
    small_received = swap(small, "dy", 1)
    pieces = split_dy(where, pieces[0], received, small, small_received, groups)
    received = [swap(pieces[k], "dy", 2 * k) for k in range(1, groups)]
    final = add_dy(where, pieces[0], received, small.shape[0])
    pieces = [final] + [swap(final, "dx", k) for k in range(1, peers)]
    return tuple(assemble(where, pieces, small.shape[0]))


def solution(mesh):
    in_specs = (P("dy", "dx", None), P("dy", "dx"), P("dy", "dx", None, None), P(), P(), P(), P())
    out_specs = (P(), P(), P("dy", None))
    return jax.shard_map(
        on_device, mesh=mesh, in_specs=in_specs, out_specs=out_specs, check_vma=False
    )
```

```python
import functools
import math

import jax
import jax.numpy as jnp
from jax import lax
from jax.experimental import pallas as pl
from jax.experimental.pallas import tpu as pltpu
from jax.sharding import PartitionSpec as P

BF16 = jnp.bfloat16
F32 = jnp.float32
LANES = 128
SMALL = 12
HALF_ROOT = 0.7071067811865476
ROWS = 32
VMEM_SPEC = pl.BlockSpec(memory_space=pltpu.VMEM)
HBM_SPEC = pl.BlockSpec(memory_space=pltpu.HBM)
SMEM_SPEC = pl.BlockSpec(memory_space=pltpu.SMEM)


def gelu_cdf(value):
    return 0.5 * (1.0 + lax.erf(value * 0.7071067811865476))


def gelu_slope(value):
    return gelu_cdf(value) + value * jnp.exp(-0.5 * value * value) * 0.3989422804014327


def in_hbm(array):
    return pltpu.with_memory_space_constraint(array, pltpu.HBM)


def rows_of(index):
    return slice(index * ROWS, (index + 1) * ROWS)


def chunk(index, rows=ROWS):
    return pl.ds(pl.multiple_of(index * rows, rows), rows)


def fold(rows):
    total = rows[0:8]
    for start in range(8, rows.shape[0], 8):
        total = total + rows[start : start + 8]
    return total


def conv_of_sum(sums, weights):
    rest, total = sums, []
    for _ in range(3):
        part = rest.astype(BF16).astype(F32)
        rest = rest - part
        total.append(part)
    total.append(jnp.zeros((5, sums.shape[1]), F32))
    lhs = jnp.concatenate(total, axis=0).astype(BF16)
    return jnp.sum(jnp.dot(lhs, weights, preferred_element_type=F32), axis=0, keepdims=True)


def forward_kernel(peers, slots, crops, frames, channels, block, loss_scale, where, *refs):
    buffers, refs = refs[:peers], refs[peers:]
    (taps, gain, bias, spread, mask, cot, second) = refs[:7]
    (keep, send, grad_rows, patches, stats) = refs[7:12]
    (waves, acc, all_rows), refs = refs[12:15], refs[15:]
    samples = 10 * (frames + 1)
    first_len = 2 * frames + 1
    long = frames + 8
    period = spread.shape[0]
    per_block = period // 10
    own = where[0]
    core = where[1]
    wanted = waves.shape[0]

    counts = [buffer[0:1, samples : samples + 1].astype(F32) for buffer in buffers]
    slot = lax.broadcasted_iota(jnp.int32, (wanted, slots), 1)
    number = lax.broadcasted_iota(jnp.int32, (wanted, slots), 0) * peers + own
    hits = []
    for k in range(peers):
        holder = jnp.bitwise_xor(own, k)
        start = jnp.zeros((1, 1), F32)
        for other in range(peers):
            before = jnp.bitwise_xor(own, other) < holder
            start = start + jnp.where(before, counts[other], 0.0)
        first = jnp.broadcast_to(start.astype(jnp.int32), (wanted, slots))
        live = jnp.broadcast_to(counts[k].astype(jnp.int32), (wanted, slots))
        hit = (first + slot == number) & (slot < live)
        hits.append(jnp.where(hit, 1.0, 0.0))
    waves[...] = jnp.dot(
        jnp.concatenate(hits, axis=1).astype(BF16),
        jnp.concatenate([buffer[...] for buffer in buffers], axis=0),
        preferred_element_type=F32,
    )
    last_row = lax.broadcasted_iota(jnp.int32, (16, LANES), 0)
    last_lane = lax.broadcasted_iota(jnp.int32, (16, LANES), 1)
    last_mask = (last_row == 0) & (last_lane < 10)
    tail_row = lax.broadcasted_iota(jnp.int32, (8, channels), 0) == 0
    steps = range(frames // ROWS)

    def scratch(crop):
        own = refs[5 * (crop % 2) : 5 * (crop % 2) + 5]
        return *own[:4], all_rows.at[crop], own[4]

    def convolve(crop):
        wave_rows, even, odd = scratch(crop)[:3]
        wave = waves[crop : crop + 1]
        pieces = []
        for part in range(10 * frames // period):
            piece = jnp.broadcast_to(wave[:, part * period : (part + 1) * period], (16, period))
            piece = jnp.concatenate([piece.astype(BF16)] * (per_block // 16), axis=0)
            pieces.append(piece * mask[...])
        wave_rows[0:frames] = jnp.dot(
            jnp.concatenate(pieces, axis=0), spread[...], preferred_element_type=F32
        )
        last = jnp.broadcast_to(wave[:, 10 * frames : 10 * frames + LANES], (16, LANES))
        wave_rows[frames : frames + 16] = jnp.where(last_mask, last, 0.0)
        both = wave_rows[0:long] + pltpu.roll(wave_rows[1 : long + 1], 10, 1)
        patch = both.astype(BF16)
        patches[crop] = patch
        yield

        sums = jnp.sum(fold(both), axis=0, keepdims=True)
        total = conv_of_sum(sums, taps[:, :channels]) + conv_of_sum(
            sums - both[frames : frames + 1], taps[:, channels:]
        )
        mean = total * (1.0 / first_len)
        centre = jnp.dot(patch, taps[:, :channels], preferred_element_type=F32) - mean
        even[...] = centre
        total = fold(centre[:frames] * centre[:frames])
        yield
        tail = centre[frames:long]
        total = total + jnp.where(tail_row, tail * tail, 0.0)
        centre = jnp.dot(patch[:frames], taps[:, channels:], preferred_element_type=F32) - mean
        odd[...] = centre
        total = total + fold(centre * centre)
        var = jnp.sum(total, axis=0, keepdims=True) * (1.0 / first_len)
        inv_std = lax.rsqrt(var + 1e-05)
        stats[crop, 0:1] = mean
        stats[crop, 1:2] = inv_std
        yield

    def hide(crop):
        _, even, odd, hid, rows, _ = scratch(crop)
        scale = stats[crop, 1:2] * gain[...] * HALF_ROOT
        shift = bias[...] * HALF_ROOT

        def hidden(centre):
            value = centre * scale + shift
            return (value * HALF_ROOT) * (1.0 + lax.erf(value))

        def late(i):
            value = hid[i * ROWS + 1 : (i + 1) * ROWS + 1]
            rows[rows_of(i), 2 * channels :] = value.astype(BF16)

        hid[frames:long] = hidden(even[frames:long])
        for i in steps:
            value = hidden(even[rows_of(i)])
            hid[rows_of(i)] = value
            rows[rows_of(i), 0:channels] = value.astype(BF16)
            value = hidden(odd[rows_of(i)])
            rows[rows_of(i), channels : 2 * channels] = value.astype(BF16)
            if i:
                late(i - 1)
            yield
        late(steps[-1])

    def middle(crop):
        rows, pre = scratch(crop)[4:6]
        pre[...] = jnp.dot(rows[...], second[...], preferred_element_type=F32)
        yield
        for i in steps:
            value = pre[rows_of(i)]
            scaled = value * HALF_ROOT
            bell = jnp.exp2((scaled * scaled) * (-1.4426950408889634))
            slope = (1.0 + lax.erf(scaled)) * (0.5 * loss_scale) + (value * bell) * (
                0.3989422804014327 * loss_scale
            )
            value = cot[crop, rows_of(i)].astype(F32) * slope
            grad_rows[crop, rows_of(i)] = value.astype(BF16)
            yield

    def outer(crop):
        swapped = core == 1
        size = acc.shape[0] // 2 if acc.shape[0] % (4 * block) == 0 else acc.shape[0]
        for low in range(0, acc.shape[0], size):
            at = slice(low, low + size)
            product = lax.dot_general(
                all_rows[crop, :, at],
                grad_rows[crop],
                (((0,), (0,)), ((), ())),
                preferred_element_type=F32,
            )
            if crop:
                product = acc[at] + product
            if crop < crops - 1:
                acc[at] = product
                yield
                continue
            for pair in range(size // (2 * block)):
                zero = product[2 * pair * block : (2 * pair + 1) * block]
                one = product[(2 * pair + 1) * block : (2 * pair + 2) * block]
                to = pl.ds(low // 2 + pair * block, block)
                keep[to] = jnp.where(swapped, one, zero)
                send[to] = jnp.where(swapped, zero, one).astype(BF16)
            yield

    def together(*streams):
        steps = []
        for stream in streams:
            steps.append((0, len(steps), stream))
        while steps:
            steps.sort(key=lambda step: step[:2])
            count, index, stream = steps.pop(0)
            if next(stream, stream) is not stream:
                steps.append((count + (10, 30, 10, 30)[index], index, stream))

    for stage in range(-2, crops + 1):
        streams = (
            (middle, stage),
            (outer, stage - 1),
            (hide, stage + 1),
            (convolve, stage + 2),
        )
        together(*[stream(crop) if 0 <= crop < crops else iter(()) for stream, crop in streams])


def forward(where, buffers, taps, gain, bias, spread, mask, cot, second, block, loss_scale):
    peers = len(buffers)
    slots, width = buffers[0].shape
    crops, frames, channels = cot.shape
    long = frames + 8
    half = second.shape[0] // 2
    per_crop = [
        pltpu.VMEM((frames + 16, LANES), F32),
        pltpu.VMEM((long, channels), F32),
        pltpu.VMEM((frames, channels), F32),
        pltpu.VMEM((long, channels), F32),
        pltpu.VMEM((frames, channels), F32),
    ]
    return pl.pallas_call(
        functools.partial(
            forward_kernel, peers, slots, crops, frames, channels, block, loss_scale
        ),
        in_specs=[SMEM_SPEC] + [VMEM_SPEC] * (peers + 7),
        out_specs=[VMEM_SPEC] * 5,
        out_shape=[
            jax.ShapeDtypeStruct((half, channels), F32),
            jax.ShapeDtypeStruct((half, channels), BF16),
            jax.ShapeDtypeStruct((crops, frames, channels), BF16),
            jax.ShapeDtypeStruct((crops, long, LANES), BF16),
            jax.ShapeDtypeStruct((crops, 8, channels), F32),
        ],
        scratch_shapes=[
            pltpu.VMEM((max(8, crops), width), F32),
            pltpu.VMEM(second.shape, F32),
            pltpu.VMEM((crops, frames, 3 * channels), BF16),
            *per_crop,
            *per_crop,
        ],
        name="forward",
        compiler_params=pltpu.CompilerParams(vmem_limit_bytes=24 << 20),
    )(where, *buffers, taps, gain, bias, spread, mask, cot, second)


def prepare_kernel(channels, first, gain, bias, cot, second, *refs):
    (taps, spread, mask), outs = refs[:3], refs[3:7]
    early, wide, sems = refs[7:]
    copies = [
        pltpu.make_async_copy(source, target, sems.at[i])
        for i, (source, target) in enumerate(
            zip((first, gain, bias, cot, second), (early, *outs))
        )
    ]
    for copy in copies:
        copy.start()
    at = lax.broadcasted_iota(jnp.int32, spread.shape, 0) % 10
    hit = at == lax.broadcasted_iota(jnp.int32, spread.shape, 1)
    spread[...] = jnp.where(hit, 1.0, 0.0).astype(BF16)
    lane = lax.broadcasted_iota(jnp.int32, mask.shape, 1)
    low = lax.broadcasted_iota(jnp.int32, mask.shape, 0) * 10
    hit = (lane >= low) & (lane < low + 10)
    mask[...] = jnp.where(hit, 1.0, 0.0).astype(BF16)
    wide[...] = jnp.zeros_like(wide)
    copies[0].wait()
    weights = early[...].astype(F32)
    wide[0:10, :channels] = weights
    wide[5:15, channels:] = weights
    taps[0:16] = wide[...].astype(BF16)
    taps[16:] = jnp.zeros((LANES - 16, 2 * channels), BF16)
    for copy in copies[1:]:
        copy.wait()


def prepare(first, gain, bias, cot, second):
    channels = first.shape[1]
    period = 5 * LANES
    shapes = [
        jax.ShapeDtypeStruct((LANES, 2 * channels), BF16),
        jax.ShapeDtypeStruct((period, LANES), BF16),
        jax.ShapeDtypeStruct((period // 10, period), BF16),
    ]
    shapes += [jax.ShapeDtypeStruct(a.shape, a.dtype) for a in (gain, bias, cot, second)]
    return pl.pallas_call(
        functools.partial(prepare_kernel, channels),
        in_specs=[HBM_SPEC] * 5,
        out_specs=[VMEM_SPEC] * 7,
        out_shape=shapes,
        scratch_shapes=[
            pltpu.VMEM(first.shape, BF16),
            pltpu.VMEM((16, 2 * channels), F32),
            pltpu.SemaphoreType.DMA((5,)),
        ],
        name="prepare",
        compiler_params=pltpu.CompilerParams(vmem_limit_bytes=8 << 20),
    )(*[in_hbm(a) for a in (first, gain, bias, cot, second)])


def backward_kernel(
    first_crop, crops, frames, channels, grad_rows, patches, stats, taps, gain, bias, second,
    *refs,
):
    small, even, odd, cols, grad_even, grad_odd, late, first_acc, gains_acc = refs[-9:]
    step = pl.program_id(0)
    crop = step + first_crop
    long = frames + 8
    first_len = 2 * frames + 1

    @pl.when(step == 0)
    def _():
        first_acc[...] = jnp.zeros_like(first_acc)
        gains_acc[...] = jnp.zeros_like(gains_acc)

    patch = patches[crop]
    even[...] = jnp.dot(patch, taps[:, :channels], preferred_element_type=F32)
    odd[...] = jnp.dot(patch[:frames], taps[:, channels:], preferred_element_type=F32)
    cols[...] = lax.dot_general(
        grad_rows[crop],
        second[: 2 * channels],
        (((1,), (1,)), ((), ())),
        preferred_element_type=F32,
    )
    late[0:8] = jnp.zeros((8, channels), F32)
    late[8 : frames + 8] = lax.dot_general(
        grad_rows[crop],
        second[2 * channels :],
        (((1,), (1,)), ((), ())),
        preferred_element_type=F32,
    )
    mean = stats[crop, 0:1]
    inv_std = stats[crop, 1:2]
    scale = gain[...]
    shift = bias[...]

    def shift_grad(pre_norm, grad_hidden):
        normed = (pre_norm - mean) * inv_std
        grad = grad_hidden * gelu_slope(normed * scale + shift)
        return normed, grad

    def first_pass(i, carry):
        shifts, gains = carry
        normed, grad = shift_grad(
            even[chunk(i)], cols[chunk(i), 0:channels] + late[pl.ds(i * ROWS + 7, ROWS), :]
        )
        even[chunk(i)] = normed
        grad_even[chunk(i)] = grad
        shifts = shifts + fold(grad)
        gains = gains + fold(grad * normed)
        normed, grad = shift_grad(odd[chunk(i)], cols[chunk(i), channels:])
        odd[chunk(i)] = normed
        grad_odd[chunk(i)] = grad
        return shifts + fold(grad), gains + fold(grad * normed)

    tail_row = lax.broadcasted_iota(jnp.int32, (8, channels), 0) == 0
    tail_normed, tail_grad = shift_grad(
        even[frames:long],
        jnp.broadcast_to(late[frames + 7 : frames + 8], (8, channels)),
    )
    tail_grad = jnp.where(tail_row, tail_grad, 0.0)
    carry = (tail_grad, tail_grad * tail_normed)
    for i in range(frames // ROWS):
        carry = first_pass(i, carry)
    shifts = jnp.sum(carry[0], axis=0, keepdims=True)
    gains = jnp.sum(carry[1], axis=0, keepdims=True)
    gains_acc[0:1] += gains
    gains_acc[1:2] += shifts
    shifts = shifts * (1.0 / first_len)
    gains = gains * (1.0 / first_len)
    outer = inv_std * scale

    def grad_pre(grad, normed):
        return (outer * (grad - shifts - normed * gains)).astype(BF16)

    tail_pre = jnp.where(tail_row, outer * (tail_grad - shifts - tail_normed * gains), 0.0)
    grads = [grad_pre(grad_even[chunk(i)], even[chunk(i)]) for i in range(frames // ROWS)]
    whole_even = jnp.concatenate(grads, axis=0)
    grads = [grad_pre(grad_odd[chunk(i)], odd[chunk(i)]) for i in range(frames // ROWS)]
    whole_odd = jnp.concatenate(grads, axis=0)

    def outer_sum(a, b):
        return lax.dot_general(a, b, (((0,), (0,)), ((), ())), preferred_element_type=F32)

    first_acc[0:LANES] += outer_sum(patch[:frames], whole_even) + outer_sum(
        patch[frames:long], tail_pre.astype(BF16)
    )
    first_acc[LANES:] += outer_sum(patch[:frames], whole_odd)

    @pl.when(step == crops - 1)
    def _():
        small[...] = jnp.zeros_like(small)
        small[0:10] = first_acc[0:10] + first_acc[LANES + 5 : LANES + 15]
        small[10:12] = gains_acc[0:2]
        if len(refs) > 9:
            small[...] += refs[0][...]


def backward(crop_range, grad_rows, patches, stats, taps, gain, bias, second, *so_far):
    first_crop, crops = crop_range[0], len(crop_range)
    frames, channels = grad_rows.shape[1:]
    long = frames + 8
    return pl.pallas_call(
        functools.partial(backward_kernel, first_crop, crops, frames, channels),
        grid=(crops,),
        in_specs=[VMEM_SPEC] * (7 + len(so_far)),
        out_specs=VMEM_SPEC,
        out_shape=jax.ShapeDtypeStruct((16, channels), F32),
        scratch_shapes=[
            pltpu.VMEM((long, channels), F32),
            pltpu.VMEM((frames, channels), F32),
            pltpu.VMEM((frames, 2 * channels), F32),
            pltpu.VMEM((frames, channels), F32),
            pltpu.VMEM((frames, channels), F32),
            pltpu.VMEM((long, channels), F32),
            pltpu.VMEM((2 * LANES, channels), F32),
            pltpu.VMEM((8, channels), F32),
        ],
        name="backward",
        compiler_params=pltpu.CompilerParams(vmem_limit_bytes=16 << 20),
    )(grad_rows, patches, stats, taps, gain, bias, second, *so_far)


def tree(values):
    while len(values) > 1:
        values = [values[i] + values[i + 1] for i in range(0, len(values), 2)]
    return values[0]


def swap(value, axis, key):
    return lax.ppermute(value, axis, [(i, i ^ key) for i in range(lax.axis_size(axis))])


def parts(value):
    value = value[:SMALL]
    high = value.astype(BF16).astype(F32)
    low = (value - high).astype(BF16).astype(F32)
    return jnp.concatenate([high, low], axis=0)


def kernel_call(kernel, where, arrays, out_shape, name):
    return pl.pallas_call(
        kernel,
        in_specs=[SMEM_SPEC] + [VMEM_SPEC] * len(arrays),
        out_specs=jax.tree.map(lambda _: VMEM_SPEC, out_shape),
        out_shape=out_shape,
        name=name,
        compiler_params=pltpu.CompilerParams(vmem_limit_bytes=4 << 20),
    )(where, *arrays)


def split_dx(where, keep, received, peers, block):
    half, channels = keep.shape
    groups = half // block
    rows = block // peers
    if rows % 16:
        total = (keep + received.astype(F32)).reshape(groups, peers, rows, channels)
        picked = [
            lax.dynamic_index_in_dim(total, where[0] ^ k, axis=1, keepdims=False)
            for k in range(peers)
        ]
        picked = [p.reshape(groups * rows, channels) for p in picked]
        return [picked[0]] + [p.astype(BF16) for p in picked[1:]]

    def body(where, keep, received, *outs):
        for k in range(peers):
            part = jnp.bitwise_xor(where[0], k)
            for g in range(groups):
                at = pl.ds(pl.multiple_of(g * block + part * rows, rows), rows)
                value = keep[at] + received[at].astype(F32)
                outs[k][g * rows : (g + 1) * rows] = value.astype(outs[k].dtype)

    shape = (groups * rows, channels)
    return kernel_call(
        body,
        where,
        (keep, received),
        [jax.ShapeDtypeStruct(shape, BF16 if k else F32) for k in range(peers)],
        "split_dx",
    )


def split_dy(where, own, received, small, small_received, groups):
    rows = own.shape[0] // groups
    channels = own.shape[1]
    if rows % 16:
        total = tree([own] + [r.astype(F32) for r in received])
        total = total.reshape(groups, rows, channels)
        below = parts(small + small_received)
        picked = [
            lax.dynamic_index_in_dim(total, where[2] ^ k, axis=0, keepdims=False)
            for k in range(groups)
        ]
        return [
            jnp.concatenate([p, below], axis=0).astype(BF16 if k else F32)
            for k, p in enumerate(picked)
        ]

    def body(where, own, small, small_received, *refs):
        received, outs = refs[: len(refs) - groups], refs[len(refs) - groups :]
        below = parts(small[...] + small_received[...])
        for k in range(groups):
            at = pl.ds(pl.multiple_of(jnp.bitwise_xor(where[2], k) * rows, rows), rows)
            value = tree([own[at]] + [r[at].astype(F32) for r in received])
            outs[k][:rows] = value.astype(outs[k].dtype)
            outs[k][rows:] = below.astype(outs[k].dtype)

    shape = (rows + 2 * SMALL, channels)
    return kernel_call(
        body,
        where,
        (own, small, small_received, *received),
        [jax.ShapeDtypeStruct(shape, BF16 if k else F32) for k in range(groups)],
        "split_dy",
    )


def add_dy(where, own, received):
    rows = own.shape[0] - 2 * SMALL

    def add(own, received):
        values = [own] + [r.astype(F32) for r in received]
        small = tree([v[rows : rows + SMALL] + v[rows + SMALL :] for v in values])
        return tree([v[:rows] for v in values]).astype(BF16), parts(small).astype(BF16)

    if rows % 16:
        return jnp.concatenate(add(own, received), axis=0)

    def body(where, own, *refs):
        refs[-1][:rows], refs[-1][rows:] = add(own[...], [r[...] for r in refs[:-1]])

    return kernel_call(
        body, where, (own, *received), jax.ShapeDtypeStruct(own.shape, BF16), "add_dy"
    )


def assemble(where, pieces):
    peers = len(pieces)
    rows = pieces[0].shape[0] - 2 * SMALL
    channels = pieces[0].shape[1]

    def small_sum(values):
        values = [v[rows:].astype(F32) for v in values]
        return tree([v[:SMALL] + v[SMALL:] for v in values])

    if rows % 16:
        stacked = jnp.stack([p[:rows] for p in pieces])
        order = jnp.arange(peers, dtype=jnp.int32) ^ where[0]
        second = jnp.take(stacked, order, axis=0).reshape(peers * rows, channels)
        small = small_sum(pieces)
        return small[:10], small[10:], second.astype(F32)

    def body(where, *refs):
        values, (first, gains, second) = refs[:peers], refs[peers:]
        small = small_sum([v[...] for v in values])
        first[...] = small[0:10]
        gains[...] = small[10:]
        for k in range(peers):
            at = pl.ds(pl.multiple_of(jnp.bitwise_xor(where[0], k) * rows, rows), rows)
            second[at] = values[k][0:rows].astype(F32)

    return kernel_call(
        body,
        where,
        pieces,
        [
            jax.ShapeDtypeStruct((10, channels), F32),
            jax.ShapeDtypeStruct((2, channels), F32),
            jax.ShapeDtypeStruct((peers * rows, channels), F32),
        ],
        "assemble",
    )


def pack_kernel(counts, audio, out, wave, live, sems):
    samples = audio.shape[2]
    fetch = pltpu.make_async_copy(audio.at[0], wave, sems.at[0])
    count = pltpu.make_async_copy(counts, live, sems.at[1])
    fetch.start()
    count.start()
    edge = samples // LANES * LANES
    count.wait()
    lane = lax.broadcasted_iota(jnp.int32, (wave.shape[0], out.shape[1] - edge), 1)
    fetch.wait()
    out[:, :edge] = wave[:, :edge]
    out[:, edge:samples] = wave[:, edge:]
    out[:, samples:] = jnp.where(
        lane[:, samples - edge :] == samples - edge, live[0, 0].astype(F32), 0.0
    ).astype(BF16)


def pack(audio, counts):
    slots, samples = audio.shape[1:]
    width = (samples // LANES + 1) * LANES
    return pl.pallas_call(
        pack_kernel,
        in_specs=[pl.BlockSpec(memory_space=pl.ANY), HBM_SPEC],
        out_specs=VMEM_SPEC,
        out_shape=jax.ShapeDtypeStruct((slots, width), BF16),
        scratch_shapes=[
            pltpu.VMEM((slots, samples), BF16),
            pltpu.SMEM((1, 1), jnp.int32),
            pltpu.SemaphoreType.DMA((2,)),
        ],
        name="pack",
        compiler_params=pltpu.CompilerParams(vmem_limit_bytes=4 << 20),
    )(counts, in_hbm(audio))


def on_device(audio, counts, cotangent, conv_first, norm_gain, norm_bias, conv_second):
    peers = lax.axis_size("dx")
    members = lax.axis_size("dy")
    groups = members // 2
    own = lax.axis_index("dx")
    line = lax.axis_index("dy")
    where = jnp.stack([own, line % 2, line // 2]).astype(jnp.int32)
    crops, frames, channels = cotangent.shape[1:]
    block = conv_second.shape[0] // members
    loss_scale = 1.0 / math.sqrt(peers * members * crops * frames)

    packed = pack(audio, counts)
    buffers = [packed] + [swap(packed, "dx", k) for k in range(1, peers)]
    taps, spread, mask, gain, bias, cot, second = prepare(
        conv_first,
        norm_gain.reshape(1, channels),
        norm_bias.reshape(1, channels),
        cotangent[0],
        conv_second,
    )
    keep, send, grad_rows, patches, stats = forward(
        where, buffers, taps, gain, bias, spread, mask, cot, second, block, loss_scale
    )
    received = swap(send, "dy", 1)
    saved = (grad_rows, patches, stats, taps, gain, bias, second)
    pieces = split_dx(where, keep, received, peers, block)
    received = [swap(pieces[k], "dx", k) for k in range(1, peers)]
    small = backward(range(crops), *saved)
    small_received = swap(small, "dy", 1)
    pieces = split_dy(where, pieces[0], received, small, small_received, groups)
    received = [swap(pieces[k], "dy", 2 * k) for k in range(1, groups)]
    final = add_dy(where, pieces[0], received)
    pieces = [final] + [swap(final, "dx", k) for k in range(1, peers)]
    return tuple(assemble(where, pieces))


def solution(mesh):
    in_specs = (P("dy", "dx", None), P("dy", "dx"), P("dy", "dx", None, None), P(), P(), P(), P())
    out_specs = (P(), P(), P("dy", None))
    return jax.shard_map(
        on_device, mesh=mesh, in_specs=in_specs, out_specs=out_specs, check_vma=False
    )
```

```python
import functools
import math

import jax
import jax.numpy as jnp
from jax import lax
from jax.experimental import pallas as pl
from jax.experimental.pallas import tpu as pltpu
from jax.sharding import PartitionSpec as P

BF16 = jnp.bfloat16
F32 = jnp.float32
LANES = 128
SMALL = 12
HALF_ROOT = 0.7071067811865476
ROWS = 32
VMEM_SPEC = pl.BlockSpec(memory_space=pltpu.VMEM)
HBM_SPEC = pl.BlockSpec(memory_space=pltpu.HBM)


def gelu_cdf(value):
    return 0.5 * (1.0 + lax.erf(value * 0.7071067811865476))


def gelu_slope(value):
    return gelu_cdf(value) + value * jnp.exp(-0.5 * value * value) * 0.3989422804014327


def in_hbm(array):
    return pltpu.with_memory_space_constraint(array, pltpu.HBM)


def rows_of(index):
    return slice(index * ROWS, (index + 1) * ROWS)


def chunk(index, rows=ROWS):
    return pl.ds(pl.multiple_of(index * rows, rows), rows)


def fold(rows):
    total = rows[0:8]
    for start in range(8, rows.shape[0], 8):
        total = total + rows[start : start + 8]
    return total


def conv_of_sum(sums, weights):
    rest, total = sums, []
    for _ in range(3):
        part = rest.astype(BF16).astype(F32)
        rest = rest - part
        total.append(part)
    total.append(jnp.zeros((5, sums.shape[1]), F32))
    lhs = jnp.concatenate(total, axis=0).astype(BF16)
    return jnp.sum(jnp.dot(lhs, weights, preferred_element_type=F32), axis=0, keepdims=True)


def forward_kernel(peers, slots, crops, frames, channels, block, loss_scale, *refs):
    buffers, refs = refs[:peers], refs[peers:]
    (taps, gain, bias, spread, mask, cot, second) = refs[:7]
    (keep, send, grad_rows, patches, stats) = refs[7:12]
    (waves, acc, all_rows), refs = refs[12:15], refs[15:]
    samples = 10 * (frames + 1)
    first_len = 2 * frames + 1
    long = frames + 8
    period = spread.shape[0]
    per_block = period // 10
    own, core, _ = position()
    wanted = waves.shape[0]

    counts = [buffer[0:1, samples : samples + 1].astype(F32) for buffer in buffers]
    slot = lax.broadcasted_iota(jnp.int32, (wanted, slots), 1)
    number = lax.broadcasted_iota(jnp.int32, (wanted, slots), 0) * peers + own
    hits = []
    for k in range(peers):
        holder = jnp.bitwise_xor(own, k)
        start = jnp.zeros((1, 1), F32)
        for other in range(peers):
            before = jnp.bitwise_xor(own, other) < holder
            start = start + jnp.where(before, counts[other], 0.0)
        first = jnp.broadcast_to(start.astype(jnp.int32), (wanted, slots))
        live = jnp.broadcast_to(counts[k].astype(jnp.int32), (wanted, slots))
        hit = (first + slot == number) & (slot < live)
        hits.append(jnp.where(hit, 1.0, 0.0))
    waves[...] = jnp.dot(
        jnp.concatenate(hits, axis=1).astype(BF16),
        jnp.concatenate([buffer[...] for buffer in buffers], axis=0),
        preferred_element_type=F32,
    )
    last_row = lax.broadcasted_iota(jnp.int32, (16, LANES), 0)
    last_lane = lax.broadcasted_iota(jnp.int32, (16, LANES), 1)
    last_mask = (last_row == 0) & (last_lane < 10)
    tail_row = lax.broadcasted_iota(jnp.int32, (8, channels), 0) == 0
    steps = range(frames // ROWS)

    def scratch(crop):
        own = refs[5 * (crop % 2) : 5 * (crop % 2) + 5]
        return *own[:4], all_rows.at[crop], own[4]

    def convolve(crop):
        wave_rows, even, odd = scratch(crop)[:3]
        wave = waves[crop : crop + 1]
        pieces = []
        for part in range(10 * frames // period):
            piece = jnp.broadcast_to(wave[:, part * period : (part + 1) * period], (16, period))
            piece = jnp.concatenate([piece.astype(BF16)] * (per_block // 16), axis=0)
            pieces.append(piece * mask[...])
        wave_rows[0:frames] = jnp.dot(
            jnp.concatenate(pieces, axis=0), spread[...], preferred_element_type=F32
        )
        last = jnp.broadcast_to(wave[:, 10 * frames : 10 * frames + LANES], (16, LANES))
        wave_rows[frames : frames + 16] = jnp.where(last_mask, last, 0.0)
        both = wave_rows[0:long] + pltpu.roll(wave_rows[1 : long + 1], 10, 1)
        patch = both.astype(BF16)
        patches[crop] = patch
        yield

        sums = jnp.sum(fold(both), axis=0, keepdims=True)
        total = conv_of_sum(sums, taps[:, :channels]) + conv_of_sum(
            sums - both[frames : frames + 1], taps[:, channels:]
        )
        mean = total * (1.0 / first_len)
        centre = jnp.dot(patch, taps[:, :channels], preferred_element_type=F32) - mean
        even[...] = centre
        total = fold(centre[:frames] * centre[:frames])
        yield
        tail = centre[frames:long]
        total = total + jnp.where(tail_row, tail * tail, 0.0)
        centre = jnp.dot(patch[:frames], taps[:, channels:], preferred_element_type=F32) - mean
        odd[...] = centre
        total = total + fold(centre * centre)
        var = jnp.sum(total, axis=0, keepdims=True) * (1.0 / first_len)
        inv_std = lax.rsqrt(var + 1e-05)
        stats[crop, 0:1] = mean
        stats[crop, 1:2] = inv_std
        yield

    def hide(crop):
        _, even, odd, hid, rows, _ = scratch(crop)
        scale = stats[crop, 1:2] * gain[...] * HALF_ROOT
        shift = bias[...] * HALF_ROOT

        def hidden(centre):
            value = centre * scale + shift
            return (value * HALF_ROOT) * (1.0 + lax.erf(value))

        def late(i):
            value = hid[i * ROWS + 1 : (i + 1) * ROWS + 1]
            rows[rows_of(i), 2 * channels :] = value.astype(BF16)

        hid[frames:long] = hidden(even[frames:long])
        for i in steps:
            value = hidden(even[rows_of(i)])
            hid[rows_of(i)] = value
            rows[rows_of(i), 0:channels] = value.astype(BF16)
            value = hidden(odd[rows_of(i)])
            rows[rows_of(i), channels : 2 * channels] = value.astype(BF16)
            if i:
                late(i - 1)
            yield
        late(steps[-1])

    def middle(crop):
        rows, pre = scratch(crop)[4:6]
        pre[...] = jnp.dot(rows[...], second[...], preferred_element_type=F32)
        yield
        for i in steps:
            value = pre[rows_of(i)]
            scaled = value * HALF_ROOT
            bell = jnp.exp2((scaled * scaled) * (-1.4426950408889634))
            slope = (1.0 + lax.erf(scaled)) * (0.5 * loss_scale) + (value * bell) * (
                0.3989422804014327 * loss_scale
            )
            value = cot[crop, rows_of(i)].astype(F32) * slope
            grad_rows[crop, rows_of(i)] = value.astype(BF16)
            yield

    def outer(crop):
        swapped = core == 1
        size = acc.shape[0] // 2 if acc.shape[0] % (4 * block) == 0 else acc.shape[0]
        for low in range(0, acc.shape[0], size):
            at = slice(low, low + size)
            product = lax.dot_general(
                all_rows[crop, :, at],
                grad_rows[crop],
                (((0,), (0,)), ((), ())),
                preferred_element_type=F32,
            )
            if crop:
                product = acc[at] + product
            if crop < crops - 1:
                acc[at] = product
                yield
                continue
            for pair in range(size // (2 * block)):
                zero = product[2 * pair * block : (2 * pair + 1) * block]
                one = product[(2 * pair + 1) * block : (2 * pair + 2) * block]
                to = pl.ds(low // 2 + pair * block, block)
                keep[to] = jnp.where(swapped, one, zero)
                send[to] = jnp.where(swapped, zero, one).astype(BF16)
            yield

    def together(*streams):
        steps = []
        for stream in streams:
            steps.append((0, len(steps), stream))
        while steps:
            steps.sort(key=lambda step: step[:2])
            count, index, stream = steps.pop(0)
            if next(stream, stream) is not stream:
                steps.append((count + (10, 30, 10, 30)[index], index, stream))

    for stage in range(-2, crops + 1):
        streams = (
            (middle, stage),
            (outer, stage - 1),
            (hide, stage + 1),
            (convolve, stage + 2),
        )
        together(*[stream(crop) if 0 <= crop < crops else iter(()) for stream, crop in streams])


def forward(buffers, taps, gain, bias, spread, mask, cot, second, block, loss_scale):
    peers = len(buffers)
    slots, width = buffers[0].shape
    crops, frames, channels = cot.shape
    long = frames + 8
    half = second.shape[0] // 2
    per_crop = [
        pltpu.VMEM((frames + 16, LANES), F32),
        pltpu.VMEM((long, channels), F32),
        pltpu.VMEM((frames, channels), F32),
        pltpu.VMEM((long, channels), F32),
        pltpu.VMEM((frames, channels), F32),
    ]
    return pl.pallas_call(
        functools.partial(
            forward_kernel, peers, slots, crops, frames, channels, block, loss_scale
        ),
        in_specs=[VMEM_SPEC] * (peers + 7),
        out_specs=[VMEM_SPEC] * 5,
        out_shape=[
            jax.ShapeDtypeStruct((half, channels), F32),
            jax.ShapeDtypeStruct((half, channels), BF16),
            jax.ShapeDtypeStruct((crops, frames, channels), BF16),
            jax.ShapeDtypeStruct((crops, long, LANES), BF16),
            jax.ShapeDtypeStruct((crops, 8, channels), F32),
        ],
        scratch_shapes=[
            pltpu.VMEM((max(8, crops), width), F32),
            pltpu.VMEM(second.shape, F32),
            pltpu.VMEM((crops, frames, 3 * channels), BF16),
            *per_crop,
            *per_crop,
        ],
        name="forward",
        compiler_params=pltpu.CompilerParams(vmem_limit_bytes=24 << 20),
    )(*buffers, taps, gain, bias, spread, mask, cot, second)


def prepare_kernel(channels, first, gain, bias, cot, second, *refs):
    (taps, spread, mask), outs = refs[:3], refs[3:7]
    early, wide, sems = refs[7:]
    copies = [
        pltpu.make_async_copy(source, target, sems.at[i])
        for i, (source, target) in enumerate(
            zip((first, gain, bias, cot, second), (early, *outs))
        )
    ]
    for copy in copies:
        copy.start()
    at = lax.broadcasted_iota(jnp.int32, spread.shape, 0) % 10
    hit = at == lax.broadcasted_iota(jnp.int32, spread.shape, 1)
    spread[...] = jnp.where(hit, 1.0, 0.0).astype(BF16)
    lane = lax.broadcasted_iota(jnp.int32, mask.shape, 1)
    low = lax.broadcasted_iota(jnp.int32, mask.shape, 0) * 10
    hit = (lane >= low) & (lane < low + 10)
    mask[...] = jnp.where(hit, 1.0, 0.0).astype(BF16)
    wide[...] = jnp.zeros_like(wide)
    copies[0].wait()
    weights = early[...].astype(F32)
    wide[0:10, :channels] = weights
    wide[5:15, channels:] = weights
    taps[0:16] = wide[...].astype(BF16)
    taps[16:] = jnp.zeros((LANES - 16, 2 * channels), BF16)
    for copy in copies[1:]:
        copy.wait()


def prepare(first, gain, bias, cot, second):
    channels = first.shape[1]
    period = 5 * LANES
    shapes = [
        jax.ShapeDtypeStruct((LANES, 2 * channels), BF16),
        jax.ShapeDtypeStruct((period, LANES), BF16),
        jax.ShapeDtypeStruct((period // 10, period), BF16),
    ]
    shapes += [jax.ShapeDtypeStruct(a.shape, a.dtype) for a in (gain, bias, cot, second)]
    return pl.pallas_call(
        functools.partial(prepare_kernel, channels),
        in_specs=[HBM_SPEC] * 5,
        out_specs=[VMEM_SPEC] * 7,
        out_shape=shapes,
        scratch_shapes=[
            pltpu.VMEM(first.shape, BF16),
            pltpu.VMEM((16, 2 * channels), F32),
            pltpu.SemaphoreType.DMA((5,)),
        ],
        name="prepare",
        compiler_params=pltpu.CompilerParams(vmem_limit_bytes=8 << 20),
    )(*[in_hbm(a) for a in (first, gain, bias, cot, second)])


def backward_kernel(
    first_crop, crops, frames, channels, grad_rows, patches, stats, taps, gain, bias, second,
    *refs,
):
    small, even, odd, cols, grad_even, grad_odd, late, first_acc, gains_acc = refs[-9:]
    step = pl.program_id(0)
    crop = step + first_crop
    long = frames + 8
    first_len = 2 * frames + 1

    @pl.when(step == 0)
    def _():
        first_acc[...] = jnp.zeros_like(first_acc)
        gains_acc[...] = jnp.zeros_like(gains_acc)

    patch = patches[crop]
    even[...] = jnp.dot(patch, taps[:, :channels], preferred_element_type=F32)
    odd[...] = jnp.dot(patch[:frames], taps[:, channels:], preferred_element_type=F32)
    cols[...] = lax.dot_general(
        grad_rows[crop],
        second[: 2 * channels],
        (((1,), (1,)), ((), ())),
        preferred_element_type=F32,
    )
    late[0:8] = jnp.zeros((8, channels), F32)
    late[8 : frames + 8] = lax.dot_general(
        grad_rows[crop],
        second[2 * channels :],
        (((1,), (1,)), ((), ())),
        preferred_element_type=F32,
    )
    mean = stats[crop, 0:1]
    inv_std = stats[crop, 1:2]
    scale = gain[...]
    shift = bias[...]

    def shift_grad(pre_norm, grad_hidden):
        normed = (pre_norm - mean) * inv_std
        grad = grad_hidden * gelu_slope(normed * scale + shift)
        return normed, grad

    def first_pass(i, carry):
        shifts, gains = carry
        normed, grad = shift_grad(
            even[chunk(i)], cols[chunk(i), 0:channels] + late[pl.ds(i * ROWS + 7, ROWS), :]
        )
        even[chunk(i)] = normed
        grad_even[chunk(i)] = grad
        shifts = shifts + fold(grad)
        gains = gains + fold(grad * normed)
        normed, grad = shift_grad(odd[chunk(i)], cols[chunk(i), channels:])
        odd[chunk(i)] = normed
        grad_odd[chunk(i)] = grad
        return shifts + fold(grad), gains + fold(grad * normed)

    tail_row = lax.broadcasted_iota(jnp.int32, (8, channels), 0) == 0
    tail_normed, tail_grad = shift_grad(
        even[frames:long],
        jnp.broadcast_to(late[frames + 7 : frames + 8], (8, channels)),
    )
    tail_grad = jnp.where(tail_row, tail_grad, 0.0)
    carry = (tail_grad, tail_grad * tail_normed)
    for i in range(frames // ROWS):
        carry = first_pass(i, carry)
    shifts = jnp.sum(carry[0], axis=0, keepdims=True)
    gains = jnp.sum(carry[1], axis=0, keepdims=True)
    gains_acc[0:1] += gains
    gains_acc[1:2] += shifts
    shifts = shifts * (1.0 / first_len)
    gains = gains * (1.0 / first_len)
    outer = inv_std * scale

    def grad_pre(grad, normed):
        return (outer * (grad - shifts - normed * gains)).astype(BF16)

    tail_pre = jnp.where(tail_row, outer * (tail_grad - shifts - tail_normed * gains), 0.0)
    grads = [grad_pre(grad_even[chunk(i)], even[chunk(i)]) for i in range(frames // ROWS)]
    whole_even = jnp.concatenate(grads, axis=0)
    grads = [grad_pre(grad_odd[chunk(i)], odd[chunk(i)]) for i in range(frames // ROWS)]
    whole_odd = jnp.concatenate(grads, axis=0)

    def outer_sum(a, b):
        return lax.dot_general(a, b, (((0,), (0,)), ((), ())), preferred_element_type=F32)

    first_acc[0:LANES] += outer_sum(patch[:frames], whole_even) + outer_sum(
        patch[frames:long], tail_pre.astype(BF16)
    )
    first_acc[LANES:] += outer_sum(patch[:frames], whole_odd)

    @pl.when(step == crops - 1)
    def _():
        small[...] = jnp.zeros_like(small)
        small[0:10] = first_acc[0:10] + first_acc[LANES + 5 : LANES + 15]
        small[10:12] = gains_acc[0:2]
        if len(refs) > 9:
            small[...] += refs[0][...]


def backward(crop_range, grad_rows, patches, stats, taps, gain, bias, second, *so_far):
    first_crop, crops = crop_range[0], len(crop_range)
    frames, channels = grad_rows.shape[1:]
    long = frames + 8
    return pl.pallas_call(
        functools.partial(backward_kernel, first_crop, crops, frames, channels),
        grid=(crops,),
        in_specs=[VMEM_SPEC] * (7 + len(so_far)),
        out_specs=VMEM_SPEC,
        out_shape=jax.ShapeDtypeStruct((16, channels), F32),
        scratch_shapes=[
            pltpu.VMEM((long, channels), F32),
            pltpu.VMEM((frames, channels), F32),
            pltpu.VMEM((frames, 2 * channels), F32),
            pltpu.VMEM((frames, channels), F32),
            pltpu.VMEM((frames, channels), F32),
            pltpu.VMEM((long, channels), F32),
            pltpu.VMEM((2 * LANES, channels), F32),
            pltpu.VMEM((8, channels), F32),
        ],
        name="backward",
        compiler_params=pltpu.CompilerParams(vmem_limit_bytes=16 << 20),
    )(grad_rows, patches, stats, taps, gain, bias, second, *so_far)


def tree(values):
    while len(values) > 1:
        values = [values[i] + values[i + 1] for i in range(0, len(values), 2)]
    return values[0]


def swap(value, axis, key):
    return lax.ppermute(value, axis, [(i, i ^ key) for i in range(lax.axis_size(axis))])


def parts(value):
    value = value[:SMALL]
    high = value.astype(BF16).astype(F32)
    low = (value - high).astype(BF16).astype(F32)
    return jnp.concatenate([high, low], axis=0)


def position():
    line = lax.axis_index("dy")
    return lax.axis_index("dx"), jnp.bitwise_and(line, 1), jnp.right_shift(line, 1)


def kernel_call(kernel, arrays, out_shape, name):
    return pl.pallas_call(
        kernel,
        in_specs=[VMEM_SPEC] * len(arrays),
        out_specs=jax.tree.map(lambda _: VMEM_SPEC, out_shape),
        out_shape=out_shape,
        name=name,
        compiler_params=pltpu.CompilerParams(vmem_limit_bytes=4 << 20),
    )(*arrays)


def split_dx(keep, received, peers, block):
    half, channels = keep.shape
    groups = half // block
    rows = block // peers
    if rows % 16:
        total = (keep + received.astype(F32)).reshape(groups, peers, rows, channels)
        picked = [
            lax.dynamic_index_in_dim(total, position()[0] ^ k, axis=1, keepdims=False)
            for k in range(peers)
        ]
        picked = [p.reshape(groups * rows, channels) for p in picked]
        return [picked[0]] + [p.astype(BF16) for p in picked[1:]]

    def body(keep, received, *outs):
        place = position()[0]
        for k in range(peers):
            part = jnp.bitwise_xor(place, k)
            for g in range(groups):
                at = pl.ds(pl.multiple_of(g * block + part * rows, rows), rows)
                value = keep[at] + received[at].astype(F32)
                outs[k][g * rows : (g + 1) * rows] = value.astype(outs[k].dtype)

    shape = (groups * rows, channels)
    return kernel_call(
        body,
        (keep, received),
        [jax.ShapeDtypeStruct(shape, BF16 if k else F32) for k in range(peers)],
        "split_dx",
    )


def split_dy(own, received, small, small_received, groups):
    rows = own.shape[0] // groups
    channels = own.shape[1]
    if rows % 16:
        total = tree([own] + [r.astype(F32) for r in received])
        total = total.reshape(groups, rows, channels)
        below = parts(small + small_received)
        picked = [
            lax.dynamic_index_in_dim(total, position()[2] ^ k, axis=0, keepdims=False)
            for k in range(groups)
        ]
        return [
            jnp.concatenate([p, below], axis=0).astype(BF16 if k else F32)
            for k, p in enumerate(picked)
        ]

    def body(own, small, small_received, *refs):
        received, outs = refs[: len(refs) - groups], refs[len(refs) - groups :]
        place = position()[2]
        below = parts(small[...] + small_received[...])
        for k in range(groups):
            at = pl.ds(pl.multiple_of(jnp.bitwise_xor(place, k) * rows, rows), rows)
            value = tree([own[at]] + [r[at].astype(F32) for r in received])
            outs[k][:rows] = value.astype(outs[k].dtype)
            outs[k][rows:] = below.astype(outs[k].dtype)

    shape = (rows + 2 * SMALL, channels)
    return kernel_call(
        body,
        (own, small, small_received, *received),
        [jax.ShapeDtypeStruct(shape, BF16 if k else F32) for k in range(groups)],
        "split_dy",
    )


def add_dy(own, received):
    rows = own.shape[0] - 2 * SMALL

    def add(own, received):
        values = [own] + [r.astype(F32) for r in received]
        small = tree([v[rows : rows + SMALL] + v[rows + SMALL :] for v in values])
        return tree([v[:rows] for v in values]).astype(BF16), parts(small).astype(BF16)

    if rows % 16:
        return jnp.concatenate(add(own, received), axis=0)

    def body(own, *refs):
        refs[-1][:rows], refs[-1][rows:] = add(own[...], [r[...] for r in refs[:-1]])

    return kernel_call(
        body, (own, *received), jax.ShapeDtypeStruct(own.shape, BF16), "add_dy"
    )


def assemble(pieces):
    peers = len(pieces)
    rows = pieces[0].shape[0] - 2 * SMALL
    channels = pieces[0].shape[1]

    def small_sum(values):
        values = [v[rows:].astype(F32) for v in values]
        return tree([v[:SMALL] + v[SMALL:] for v in values])

    if rows % 16:
        stacked = jnp.stack([p[:rows] for p in pieces])
        order = jnp.arange(peers, dtype=jnp.int32) ^ position()[0]
        second = jnp.take(stacked, order, axis=0).reshape(peers * rows, channels)
        small = small_sum(pieces)
        return small[:10], small[10:], second.astype(F32)

    def body(*refs):
        values, (first, gains, second) = refs[:peers], refs[peers:]
        small = small_sum([v[...] for v in values])
        first[...] = small[0:10]
        gains[...] = small[10:]
        place = position()[0]
        for k in range(peers):
            at = pl.ds(pl.multiple_of(jnp.bitwise_xor(place, k) * rows, rows), rows)
            second[at] = values[k][0:rows].astype(F32)

    return kernel_call(
        body,
        pieces,
        [
            jax.ShapeDtypeStruct((10, channels), F32),
            jax.ShapeDtypeStruct((2, channels), F32),
            jax.ShapeDtypeStruct((peers * rows, channels), F32),
        ],
        "assemble",
    )


def pack_kernel(counts, audio, out, wave, live, sems):
    samples = audio.shape[2]
    fetch = pltpu.make_async_copy(audio.at[0], wave, sems.at[0])
    count = pltpu.make_async_copy(counts, live, sems.at[1])
    fetch.start()
    count.start()
    edge = samples // LANES * LANES
    count.wait()
    lane = lax.broadcasted_iota(jnp.int32, (wave.shape[0], out.shape[1] - edge), 1)
    fetch.wait()
    out[:, :edge] = wave[:, :edge]
    out[:, edge:samples] = wave[:, edge:]
    out[:, samples:] = jnp.where(
        lane[:, samples - edge :] == samples - edge, live[0, 0].astype(F32), 0.0
    ).astype(BF16)


def pack(audio, counts):
    slots, samples = audio.shape[1:]
    width = (samples // LANES + 1) * LANES
    return pl.pallas_call(
        pack_kernel,
        in_specs=[pl.BlockSpec(memory_space=pl.ANY), HBM_SPEC],
        out_specs=VMEM_SPEC,
        out_shape=jax.ShapeDtypeStruct((slots, width), BF16),
        scratch_shapes=[
            pltpu.VMEM((slots, samples), BF16),
            pltpu.SMEM((1, 1), jnp.int32),
            pltpu.SemaphoreType.DMA((2,)),
        ],
        name="pack",
        compiler_params=pltpu.CompilerParams(vmem_limit_bytes=4 << 20),
    )(counts, in_hbm(audio))


def on_device(audio, counts, cotangent, conv_first, norm_gain, norm_bias, conv_second):
    peers = lax.axis_size("dx")
    members = lax.axis_size("dy")
    groups = members // 2
    crops, frames, channels = cotangent.shape[1:]
    block = conv_second.shape[0] // members
    loss_scale = 1.0 / math.sqrt(peers * members * crops * frames)

    packed = pack(audio, counts)
    buffers = [packed] + [swap(packed, "dx", k) for k in range(1, peers)]
    taps, spread, mask, gain, bias, cot, second = prepare(
        conv_first,
        norm_gain.reshape(1, channels),
        norm_bias.reshape(1, channels),
        cotangent[0],
        conv_second,
    )
    keep, send, grad_rows, patches, stats = forward(
        buffers, taps, gain, bias, spread, mask, cot, second, block, loss_scale
    )
    received = swap(send, "dy", 1)
    saved = (grad_rows, patches, stats, taps, gain, bias, second)
    pieces = split_dx(keep, received, peers, block)
    received = [swap(pieces[k], "dx", k) for k in range(1, peers)]
    small = backward(range(crops), *saved)
    small_received = swap(small, "dy", 1)
    pieces = split_dy(pieces[0], received, small, small_received, groups)
    received = [swap(pieces[k], "dy", 2 * k) for k in range(1, groups)]
    final = add_dy(pieces[0], received)
    pieces = [final] + [swap(final, "dx", k) for k in range(1, peers)]
    return tuple(assemble(pieces))


def solution(mesh):
    in_specs = (P("dy", "dx", None), P("dy", "dx"), P("dy", "dx", None, None), P(), P(), P(), P())
    out_specs = (P(), P(), P("dy", None))
    return jax.shard_map(
        on_device, mesh=mesh, in_specs=in_specs, out_specs=out_specs, check_vma=False
    )
```

```python
import functools
import math

import jax
import jax.numpy as jnp
from jax import lax
from jax.experimental import pallas as pl
from jax.experimental.pallas import tpu as pltpu
from jax.sharding import PartitionSpec as P

BF16 = jnp.bfloat16
F32 = jnp.float32
LANES = 128
SMALL = 12
HALF_ROOT = 0.7071067811865476
ROWS = 32
VMEM_SPEC = pl.BlockSpec(memory_space=pltpu.VMEM)
HBM_SPEC = pl.BlockSpec(memory_space=pltpu.HBM)


def gelu_cdf(value):
    return 0.5 * (1.0 + lax.erf(value * 0.7071067811865476))


def gelu_slope(value):
    return gelu_cdf(value) + value * jnp.exp(-0.5 * value * value) * 0.3989422804014327


def in_hbm(array):
    return pltpu.with_memory_space_constraint(array, pltpu.HBM)


def rows_of(index):
    return slice(index * ROWS, (index + 1) * ROWS)


def chunk(index, rows=ROWS):
    return pl.ds(pl.multiple_of(index * rows, rows), rows)


def fold(rows):
    total = rows[0:8]
    for start in range(8, rows.shape[0], 8):
        total = total + rows[start : start + 8]
    return total


def conv_of_sum(sums, weights):
    rest, total = sums, []
    for _ in range(3):
        part = rest.astype(BF16).astype(F32)
        rest = rest - part
        total.append(part)
    total.append(jnp.zeros((5, sums.shape[1]), F32))
    lhs = jnp.concatenate(total, axis=0).astype(BF16)
    return jnp.sum(jnp.dot(lhs, weights, preferred_element_type=F32), axis=0, keepdims=True)


def forward_kernel(peers, slots, crops, frames, channels, block, loss_scale, *refs):
    buffers, refs = refs[:peers], refs[peers:]
    (taps, gain, bias, spread, mask, cot, second) = refs[:7]
    (keep, send, grad_rows, patches, stats, evens, odds) = refs[7:14]
    (waves, acc, all_rows), refs = refs[14:17], refs[17:]
    samples = 10 * (frames + 1)
    first_len = 2 * frames + 1
    long = frames + 8
    period = spread.shape[0]
    per_block = period // 10
    own, core, _ = position()
    wanted = waves.shape[0]

    counts = [buffer[0:1, samples : samples + 1].astype(F32) for buffer in buffers]
    slot = lax.broadcasted_iota(jnp.int32, (wanted, slots), 1)
    number = lax.broadcasted_iota(jnp.int32, (wanted, slots), 0) * peers + own
    hits = []
    for k in range(peers):
        holder = jnp.bitwise_xor(own, k)
        start = jnp.zeros((1, 1), F32)
        for other in range(peers):
            before = jnp.bitwise_xor(own, other) < holder
            start = start + jnp.where(before, counts[other], 0.0)
        first = jnp.broadcast_to(start.astype(jnp.int32), (wanted, slots))
        live = jnp.broadcast_to(counts[k].astype(jnp.int32), (wanted, slots))
        hit = (first + slot == number) & (slot < live)
        hits.append(jnp.where(hit, 1.0, 0.0))
    waves[...] = jnp.dot(
        jnp.concatenate(hits, axis=1).astype(BF16),
        jnp.concatenate([buffer[...] for buffer in buffers], axis=0),
        preferred_element_type=F32,
    )
    last_row = lax.broadcasted_iota(jnp.int32, (16, LANES), 0)
    last_lane = lax.broadcasted_iota(jnp.int32, (16, LANES), 1)
    last_mask = (last_row == 0) & (last_lane < 10)
    tail_row = lax.broadcasted_iota(jnp.int32, (8, channels), 0) == 0
    steps = range(frames // ROWS)

    def scratch(crop):
        wave_rows, hid, pre = refs[3 * (crop % 2) : 3 * (crop % 2) + 3]
        return wave_rows, evens.at[crop], odds.at[crop], hid, all_rows.at[crop], pre

    def convolve(crop):
        wave_rows, even, odd = scratch(crop)[:3]
        wave = waves[crop : crop + 1]
        pieces = []
        for part in range(10 * frames // period):
            piece = jnp.broadcast_to(wave[:, part * period : (part + 1) * period], (16, period))
            piece = jnp.concatenate([piece.astype(BF16)] * (per_block // 16), axis=0)
            pieces.append(piece * mask[...])
        wave_rows[0:frames] = jnp.dot(
            jnp.concatenate(pieces, axis=0), spread[...], preferred_element_type=F32
        )
        last = jnp.broadcast_to(wave[:, 10 * frames : 10 * frames + LANES], (16, LANES))
        wave_rows[frames : frames + 16] = jnp.where(last_mask, last, 0.0)
        both = wave_rows[0:long] + pltpu.roll(wave_rows[1 : long + 1], 10, 1)
        patch = both.astype(BF16)
        patches[crop] = patch
        yield

        sums = jnp.sum(fold(both), axis=0, keepdims=True)
        total = conv_of_sum(sums, taps[:, :channels]) + conv_of_sum(
            sums - both[frames : frames + 1], taps[:, channels:]
        )
        mean = total * (1.0 / first_len)
        centre = jnp.dot(patch, taps[:, :channels], preferred_element_type=F32) - mean
        even[...] = centre
        total = fold(centre[:frames] * centre[:frames])
        yield
        tail = centre[frames:long]
        total = total + jnp.where(tail_row, tail * tail, 0.0)
        centre = jnp.dot(patch[:frames], taps[:, channels:], preferred_element_type=F32) - mean
        odd[...] = centre
        total = total + fold(centre * centre)
        var = jnp.sum(total, axis=0, keepdims=True) * (1.0 / first_len)
        inv_std = lax.rsqrt(var + 1e-05)
        stats[crop, 0:1] = mean
        stats[crop, 1:2] = inv_std
        yield

    def hide(crop):
        _, even, odd, hid, rows, _ = scratch(crop)
        scale = stats[crop, 1:2] * gain[...] * HALF_ROOT
        shift = bias[...] * HALF_ROOT

        def hidden(centre):
            value = centre * scale + shift
            return (value * HALF_ROOT) * (1.0 + lax.erf(value))

        def late(i):
            value = hid[i * ROWS + 1 : (i + 1) * ROWS + 1]
            rows[rows_of(i), 2 * channels :] = value.astype(BF16)

        hid[frames:long] = hidden(even[frames:long])
        for i in steps:
            value = hidden(even[rows_of(i)])
            hid[rows_of(i)] = value
            rows[rows_of(i), 0:channels] = value.astype(BF16)
            value = hidden(odd[rows_of(i)])
            rows[rows_of(i), channels : 2 * channels] = value.astype(BF16)
            if i:
                late(i - 1)
            yield
        late(steps[-1])

    def middle(crop):
        rows, pre = scratch(crop)[4:6]
        pre[...] = jnp.dot(rows[...], second[...], preferred_element_type=F32)
        yield
        for i in steps:
            value = pre[rows_of(i)]
            scaled = value * HALF_ROOT
            bell = jnp.exp2((scaled * scaled) * (-1.4426950408889634))
            slope = (1.0 + lax.erf(scaled)) * (0.5 * loss_scale) + (value * bell) * (
                0.3989422804014327 * loss_scale
            )
            value = cot[crop, rows_of(i)].astype(F32) * slope
            grad_rows[crop, rows_of(i)] = value.astype(BF16)
            yield

    def outer(crop):
        swapped = core == 1
        size = acc.shape[0] // 2 if acc.shape[0] % (4 * block) == 0 else acc.shape[0]
        for low in range(0, acc.shape[0], size):
            at = slice(low, low + size)
            product = lax.dot_general(
                all_rows[crop, :, at],
                grad_rows[crop],
                (((0,), (0,)), ((), ())),
                preferred_element_type=F32,
            )
            if crop:
                product = acc[at] + product
            if crop < crops - 1:
                acc[at] = product
                yield
                continue
            for pair in range(size // (2 * block)):
                zero = product[2 * pair * block : (2 * pair + 1) * block]
                one = product[(2 * pair + 1) * block : (2 * pair + 2) * block]
                to = pl.ds(low // 2 + pair * block, block)
                keep[to] = jnp.where(swapped, one, zero)
                send[to] = jnp.where(swapped, zero, one).astype(BF16)
            yield

    def together(*streams):
        steps = []
        for stream in streams:
            steps.append((0, len(steps), stream))
        while steps:
            steps.sort(key=lambda step: step[:2])
            count, index, stream = steps.pop(0)
            if next(stream, stream) is not stream:
                steps.append((count + (10, 30, 10, 30)[index], index, stream))

    for stage in range(-2, crops + 1):
        streams = (
            (middle, stage),
            (outer, stage - 1),
            (hide, stage + 1),
            (convolve, stage + 2),
        )
        together(*[stream(crop) if 0 <= crop < crops else iter(()) for stream, crop in streams])


def forward(buffers, taps, gain, bias, spread, mask, cot, second, block, loss_scale):
    peers = len(buffers)
    slots, width = buffers[0].shape
    crops, frames, channels = cot.shape
    long = frames + 8
    half = second.shape[0] // 2
    per_crop = [
        pltpu.VMEM((frames + 16, LANES), F32),
        pltpu.VMEM((long, channels), F32),
        pltpu.VMEM((frames, channels), F32),
    ]
    return pl.pallas_call(
        functools.partial(
            forward_kernel, peers, slots, crops, frames, channels, block, loss_scale
        ),
        in_specs=[VMEM_SPEC] * (peers + 7),
        out_specs=[VMEM_SPEC] * 7,
        out_shape=[
            jax.ShapeDtypeStruct((half, channels), F32),
            jax.ShapeDtypeStruct((half, channels), BF16),
            jax.ShapeDtypeStruct((crops, frames, channels), BF16),
            jax.ShapeDtypeStruct((crops, long, LANES), BF16),
            jax.ShapeDtypeStruct((crops, 8, channels), F32),
            jax.ShapeDtypeStruct((crops, long, channels), F32),
            jax.ShapeDtypeStruct((crops, frames, channels), F32),
        ],
        scratch_shapes=[
            pltpu.VMEM((max(8, crops), width), F32),
            pltpu.VMEM(second.shape, F32),
            pltpu.VMEM((crops, frames, 3 * channels), BF16),
            *per_crop,
            *per_crop,
        ],
        name="forward",
        compiler_params=pltpu.CompilerParams(vmem_limit_bytes=24 << 20),
    )(*buffers, taps, gain, bias, spread, mask, cot, second)


def prepare_kernel(channels, first, gain, bias, cot, second, *refs):
    (taps, spread, mask), outs = refs[:3], refs[3:7]
    early, wide, sems = refs[7:]
    copies = [
        pltpu.make_async_copy(source, target, sems.at[i])
        for i, (source, target) in enumerate(
            zip((first, gain, bias, cot, second), (early, *outs))
        )
    ]
    for copy in copies:
        copy.start()
    at = lax.broadcasted_iota(jnp.int32, spread.shape, 0) % 10
    hit = at == lax.broadcasted_iota(jnp.int32, spread.shape, 1)
    spread[...] = jnp.where(hit, 1.0, 0.0).astype(BF16)
    lane = lax.broadcasted_iota(jnp.int32, mask.shape, 1)
    low = lax.broadcasted_iota(jnp.int32, mask.shape, 0) * 10
    hit = (lane >= low) & (lane < low + 10)
    mask[...] = jnp.where(hit, 1.0, 0.0).astype(BF16)
    wide[...] = jnp.zeros_like(wide)
    copies[0].wait()
    weights = early[...].astype(F32)
    wide[0:10, :channels] = weights
    wide[5:15, channels:] = weights
    taps[0:16] = wide[...].astype(BF16)
    taps[16:] = jnp.zeros((LANES - 16, 2 * channels), BF16)
    for copy in copies[1:]:
        copy.wait()


def prepare(first, gain, bias, cot, second):
    channels = first.shape[1]
    period = 5 * LANES
    shapes = [
        jax.ShapeDtypeStruct((LANES, 2 * channels), BF16),
        jax.ShapeDtypeStruct((period, LANES), BF16),
        jax.ShapeDtypeStruct((period // 10, period), BF16),
    ]
    shapes += [jax.ShapeDtypeStruct(a.shape, a.dtype) for a in (gain, bias, cot, second)]
    return pl.pallas_call(
        functools.partial(prepare_kernel, channels),
        in_specs=[HBM_SPEC] * 5,
        out_specs=[VMEM_SPEC] * 7,
        out_shape=shapes,
        scratch_shapes=[
            pltpu.VMEM(first.shape, BF16),
            pltpu.VMEM((16, 2 * channels), F32),
            pltpu.SemaphoreType.DMA((5,)),
        ],
        name="prepare",
        compiler_params=pltpu.CompilerParams(vmem_limit_bytes=8 << 20),
    )(*[in_hbm(a) for a in (first, gain, bias, cot, second)])


def backward_kernel(
    crops, frames, channels, grad_rows, patches, stats, evens, odds, gain, bias, second, *refs
):
    extras, refs = refs[: len(refs) - 3 - 4 * len(crops)], refs[len(refs) - 3 - 4 * len(crops) :]
    small, first_acc, gains_acc = refs[:3]
    long = frames + 8
    first_len = 2 * frames + 1
    steps = range(frames // ROWS)
    tail_row = lax.broadcasted_iota(jnp.int32, (8, channels), 0) == 0
    late_rows = [slice(i * ROWS + 7, (i + 1) * ROWS + 7) for i in steps]

    def outer_sum(a, b):
        return lax.dot_general(a, b, (((0,), (0,)), ((), ())), preferred_element_type=F32)

    def scratch(crop):
        index = 3 + 4 * (crop - crops[0])
        return refs[index : index + 4]

    for crop in crops:
        cols, late = scratch(crop)[:2]
        transposed = (((1,), (1,)), ((), ()))
        cols[...] = lax.dot_general(
            grad_rows[crop], second[: 2 * channels], transposed, preferred_element_type=F32
        )
        late[0:8] = jnp.zeros((8, channels), F32)
        late[8:] = lax.dot_general(
            grad_rows[crop], second[2 * channels :], transposed, preferred_element_type=F32
        )

    for index, crop in enumerate(crops):
        cols, late, grad_even, grad_odd = scratch(crop)
        inv_std = stats[crop, 1:2]
        scale = inv_std * gain[...] * HALF_ROOT
        shift = bias[...] * HALF_ROOT

        def doubled(centre, grad_hidden):
            value = centre * scale + shift
            bell = jnp.exp2((value * value) * (-1.4426950408889634))
            slope = (1.0 + lax.erf(value)) + (value * 1.1283791670955126) * bell
            return grad_hidden * slope

        centre = evens[crop, frames:long]
        tail = doubled(centre, jnp.broadcast_to(late[long - 1 : long], (8, channels)))
        tail = jnp.where(tail_row, tail, 0.0)
        shifts, gains = tail, tail * centre
        for i in steps:
            centre = evens[crop, rows_of(i)]
            grad = doubled(centre, cols[rows_of(i), :channels] + late[late_rows[i]])
            grad_even[rows_of(i)] = grad
            shifts = shifts + fold(grad)
            gains = gains + fold(grad * centre)
            centre = odds[crop, rows_of(i)]
            grad = doubled(centre, cols[rows_of(i), channels:])
            grad_odd[rows_of(i)] = grad
            shifts = shifts + fold(grad)
            gains = gains + fold(grad * centre)
        shifts = jnp.sum(shifts, axis=0, keepdims=True)
        gains = jnp.sum(gains, axis=0, keepdims=True) * inv_std
        sums = jnp.concatenate([gains * 0.5, shifts * 0.5], axis=0)
        gains_acc[0:2] = gains_acc[0:2] + sums if index else sums
        shifts = shifts * (1.0 / first_len)
        gains = gains * inv_std * (1.0 / first_len)
        outer = 0.5 * inv_std * gain[...]

        def grad_pre(grad, centre):
            return (grad - shifts - centre * gains) * outer

        tail = jnp.where(tail_row, grad_pre(tail, evens[crop, frames:long]), 0.0)
        pieces = [grad_pre(grad_even[rows_of(i)], evens[crop, rows_of(i)]) for i in steps]
        pieces = [piece.astype(BF16) for piece in pieces]
        first = outer_sum(patches[crop, :frames], jnp.concatenate(pieces, axis=0))
        first = first + outer_sum(patches[crop, frames:long], tail.astype(BF16))
        pieces = [grad_pre(grad_odd[rows_of(i)], odds[crop, rows_of(i)]) for i in steps]
        pieces = [piece.astype(BF16) for piece in pieces]
        last = outer_sum(patches[crop, :frames], jnp.concatenate(pieces, axis=0))
        first, last = first[:16], last[:16]
        first_acc[0:16] = first_acc[0:16] + first if index else first
        first_acc[16:32] = first_acc[16:32] + last if index else last

    small[...] = jnp.zeros_like(small)
    small[0:10] = first_acc[0:10] + first_acc[21:31]
    small[10:12] = gains_acc[0:2]
    if extras:
        small[...] += extras[0][...]


def backward(crops, saved, *extras):
    grad_rows = saved[0]
    frames, channels = grad_rows.shape[1:]
    per_crop = [
        pltpu.VMEM((frames, 2 * channels), F32),
        pltpu.VMEM((frames + 8, channels), F32),
        pltpu.VMEM((frames, channels), F32),
        pltpu.VMEM((frames, channels), F32),
    ]
    return pl.pallas_call(
        functools.partial(backward_kernel, crops, frames, channels),
        in_specs=[VMEM_SPEC] * (len(saved) + len(extras)),
        out_specs=VMEM_SPEC,
        out_shape=jax.ShapeDtypeStruct((16, channels), F32),
        scratch_shapes=[
            pltpu.VMEM((32, channels), F32),
            pltpu.VMEM((8, channels), F32),
            *per_crop * len(crops),
        ],
        name="backward",
        compiler_params=pltpu.CompilerParams(vmem_limit_bytes=16 << 20),
    )(*saved, *extras)


def tree(values):
    while len(values) > 1:
        values = [values[i] + values[i + 1] for i in range(0, len(values), 2)]
    return values[0]


def swap(value, axis, key):
    return lax.ppermute(value, axis, [(i, i ^ key) for i in range(lax.axis_size(axis))])


def parts(value):
    value = value[:SMALL]
    high = value.astype(BF16).astype(F32)
    low = (value - high).astype(BF16).astype(F32)
    return jnp.concatenate([high, low], axis=0)


def position():
    line = lax.axis_index("dy")
    return lax.axis_index("dx"), jnp.bitwise_and(line, 1), jnp.right_shift(line, 1)


def kernel_call(kernel, arrays, out_shape, name):
    return pl.pallas_call(
        kernel,
        in_specs=[VMEM_SPEC] * len(arrays),
        out_specs=jax.tree.map(lambda _: VMEM_SPEC, out_shape),
        out_shape=out_shape,
        name=name,
        compiler_params=pltpu.CompilerParams(vmem_limit_bytes=4 << 20),
    )(*arrays)


def split_dx(keep, received, peers, block):
    half, channels = keep.shape
    groups = half // block
    rows = block // peers
    if rows % 16:
        total = (keep + received.astype(F32)).reshape(groups, peers, rows, channels)
        picked = [
            lax.dynamic_index_in_dim(total, position()[0] ^ k, axis=1, keepdims=False)
            for k in range(peers)
        ]
        picked = [p.reshape(groups * rows, channels) for p in picked]
        return [picked[0]] + [p.astype(BF16) for p in picked[1:]]

    def body(keep, received, *outs):
        place = position()[0]
        for k in range(peers):
            part = jnp.bitwise_xor(place, k)
            for g in range(groups):
                at = pl.ds(pl.multiple_of(g * block + part * rows, rows), rows)
                value = keep[at] + received[at].astype(F32)
                outs[k][g * rows : (g + 1) * rows] = value.astype(outs[k].dtype)

    shape = (groups * rows, channels)
    return kernel_call(
        body,
        (keep, received),
        [jax.ShapeDtypeStruct(shape, BF16 if k else F32) for k in range(peers)],
        "split_dx",
    )


def halve_dx(total_keep, received, block):
    half, channels = total_keep.shape
    groups = half // block
    rows = block // 4

    def body(keep, received, own, later, onward, near):
        place, core, _ = position()
        first, second = 1 + core, 2 - core
        for out, key in ((onward, 3), (near, first), (later, second), (own, 0)):
            part = jnp.bitwise_xor(place, key) * rows
            for g in range(groups):
                at = pl.ds(pl.multiple_of(g * block + part, rows), rows)
                value = keep[at] + received[at].astype(F32)
                out[g * rows : (g + 1) * rows] = value.astype(out.dtype)

    shape = (groups * rows, channels)
    return kernel_call(
        body,
        (total_keep, received),
        [jax.ShapeDtypeStruct(shape, kind) for kind in (F32, F32, BF16, BF16)],
        "halve_dx",
    )


def combine(later, received, _):
    def body(later, received, _, out):
        out[...] = (later[...] + received[...].astype(F32)).astype(BF16)

    return kernel_call(
        body, (later, received, _), jax.ShapeDtypeStruct(later.shape, BF16), "combine"
    )


def swap_by_core(value, keys):
    peers, members = lax.axis_size("dx"), lax.axis_size("dy")
    pairs = [
        (i * members + j, (i ^ keys[j % 2]) * members + j)
        for i in range(peers)
        for j in range(members)
    ]
    return lax.ppermute(value, ("dx", "dy"), pairs)


def split_dy(own, received, small, small_received, groups):
    rows = own.shape[0] // groups
    channels = own.shape[1]
    if rows % 16:
        total = sum([r.astype(F32) for r in received], own)
        total = total.reshape(groups, rows, channels)
        below = parts(small + small_received)
        picked = [
            lax.dynamic_index_in_dim(total, position()[2] ^ k, axis=0, keepdims=False)
            for k in range(groups)
        ]
        return [
            jnp.concatenate([p, below], axis=0).astype(BF16 if k else F32)
            for k, p in enumerate(picked)
        ]

    def body(own, small, small_received, *refs):
        received, outs = refs[: len(refs) - groups], refs[len(refs) - groups :]
        place = position()[2]
        below = parts(small[...] + small_received[...])
        for k in range(groups):
            at = pl.ds(pl.multiple_of(jnp.bitwise_xor(place, k) * rows, rows), rows)
            value = own[at]
            for r in received:
                value = value + r[at].astype(F32)
            outs[k][:rows] = value.astype(outs[k].dtype)
            outs[k][rows:] = below.astype(outs[k].dtype)

    shape = (rows + 2 * SMALL, channels)
    return kernel_call(
        body,
        (own, small, small_received, *received),
        [jax.ShapeDtypeStruct(shape, BF16 if k else F32) for k in range(groups)],
        "split_dy",
    )


def add_dy(own, received):
    rows = own.shape[0] - 2 * SMALL

    def add(own, received):
        values = [own] + [r.astype(F32) for r in received]
        small = tree([v[rows : rows + SMALL] + v[rows + SMALL :] for v in values])
        return tree([v[:rows] for v in values]).astype(BF16), parts(small).astype(BF16)

    if rows % 16:
        return jnp.concatenate(add(own, received), axis=0)

    def body(own, *refs):
        refs[-1][:rows], refs[-1][rows:] = add(own[...], [r[...] for r in refs[:-1]])

    return kernel_call(
        body, (own, *received), jax.ShapeDtypeStruct(own.shape, BF16), "add_dy"
    )


def assemble(pieces):
    peers = len(pieces)
    rows = pieces[0].shape[0] - 2 * SMALL
    channels = pieces[0].shape[1]

    def small_sum(values):
        values = [v[rows:].astype(F32) for v in values]
        return tree([v[:SMALL] + v[SMALL:] for v in values])

    if rows % 16:
        stacked = jnp.stack([p[:rows] for p in pieces])
        order = jnp.arange(peers, dtype=jnp.int32) ^ position()[0]
        second = jnp.take(stacked, order, axis=0).reshape(peers * rows, channels)
        small = small_sum(pieces)
        return small[:10], small[10:], second.astype(F32)

    def body(*refs):
        values, (first, gains, second) = refs[:peers], refs[peers:]
        small = small_sum([v[...] for v in values])
        first[...] = small[0:10]
        gains[...] = small[10:]
        place = position()[0]
        for k in range(peers):
            at = pl.ds(pl.multiple_of(jnp.bitwise_xor(place, k) * rows, rows), rows)
            second[at] = values[k][0:rows].astype(F32)

    return kernel_call(
        body,
        pieces,
        [
            jax.ShapeDtypeStruct((10, channels), F32),
            jax.ShapeDtypeStruct((2, channels), F32),
            jax.ShapeDtypeStruct((peers * rows, channels), F32),
        ],
        "assemble",
    )


def pack_kernel(counts, audio, out, wave, live, sems):
    samples = audio.shape[2]
    fetch = pltpu.make_async_copy(audio.at[0], wave, sems.at[0])
    count = pltpu.make_async_copy(counts, live, sems.at[1])
    fetch.start()
    count.start()
    edge = samples // LANES * LANES
    count.wait()
    lane = lax.broadcasted_iota(jnp.int32, (wave.shape[0], out.shape[1] - edge), 1)
    fetch.wait()
    out[:, :edge] = wave[:, :edge]
    out[:, edge:samples] = wave[:, edge:]
    out[:, samples:] = jnp.where(
        lane[:, samples - edge :] == samples - edge, live[0, 0].astype(F32), 0.0
    ).astype(BF16)


def pack(audio, counts):
    slots, samples = audio.shape[1:]
    width = (samples // LANES + 1) * LANES
    return pl.pallas_call(
        pack_kernel,
        in_specs=[pl.BlockSpec(memory_space=pl.ANY), HBM_SPEC],
        out_specs=VMEM_SPEC,
        out_shape=jax.ShapeDtypeStruct((slots, width), BF16),
        scratch_shapes=[
            pltpu.VMEM((slots, samples), BF16),
            pltpu.SMEM((1, 1), jnp.int32),
            pltpu.SemaphoreType.DMA((2,)),
        ],
        name="pack",
        compiler_params=pltpu.CompilerParams(vmem_limit_bytes=4 << 20),
    )(counts, in_hbm(audio))


def on_device(audio, counts, cotangent, conv_first, norm_gain, norm_bias, conv_second):
    peers = lax.axis_size("dx")
    members = lax.axis_size("dy")
    groups = members // 2
    crops, frames, channels = cotangent.shape[1:]
    block = conv_second.shape[0] // members
    loss_scale = 1.0 / math.sqrt(peers * members * crops * frames)

    packed = pack(audio, counts)
    buffers = [packed] + [swap(packed, "dx", k) for k in range(1, peers)]
    taps, spread, mask, gain, bias, cot, second = prepare(
        conv_first,
        norm_gain.reshape(1, channels),
        norm_bias.reshape(1, channels),
        cotangent[0],
        conv_second,
    )
    keep, send, *saved = forward(
        buffers, taps, gain, bias, spread, mask, cot, second, block, loss_scale
    )
    received = swap(send, "dy", 1)
    saved = (*saved, gain, bias, second)
    if peers == 4 and block % 64 == 0:
        own, later, onward, near = halve_dx(keep, received, block)
        onward = swap_by_core(onward, (1, 2))
        near = swap_by_core(near, (1, 2))
        small = backward(range(crops // 2), saved)
        later = combine(later, onward, small)
        received = [near, swap_by_core(later, (2, 1))]
        small = backward(range(crops // 2, crops), saved, small, later)
    else:
        own, *pieces = split_dx(keep, received, peers, block)
        received = [swap(p, "dx", k + 1) for k, p in enumerate(pieces)]
        small = backward(range(crops), saved)
    small_received = swap(small, "dy", 1)
    pieces = split_dy(own, received, small, small_received, groups)
    received = [swap(pieces[k], "dy", 2 * k) for k in range(1, groups)]
    final = add_dy(pieces[0], received)
    pieces = [final] + [swap(final, "dx", k) for k in range(1, peers)]
    return tuple(assemble(pieces))


def solution(mesh):
    in_specs = (P("dy", "dx", None), P("dy", "dx"), P("dy", "dx", None, None), P(), P(), P(), P())
    out_specs = (P(), P(), P("dy", None))
    return jax.shard_map(
        on_device, mesh=mesh, in_specs=in_specs, out_specs=out_specs, check_vma=False
    )
```
